32 devices in a mesh: dp: 8 (over y, x, core), mp: 4 (over z).
Axes of the slice: x: 2, y: 2, z: 4, core: 2. Of those that a mesh axis runs over, the one named last changes fastest.
Arguments:
- tokens: bfloat16 [8192, 1152], P(('dp', 'mp')), may hold values from -6 to 6
- conditioning: bfloat16 [32, 1152], P(('dp', 'mp')), may hold values from -6 to 6
- routes: int32 [32, 256], P(('dp', 'mp')), may hold values from 0 to 255, each once within a row
- keep_count: int32 [32], P(('dp', 'mp')), may hold values from 64 to 192, as said below
- cotangent: bfloat16 [8192, 1152], P(('dp', 'mp')), may hold values from -6 to 6
- ada_weight: bfloat16 [6912, 1152], replicated, may hold values from -0.1875 to 0.1875
- ada_bias: bfloat16 [6912], replicated, may hold values from -3 to 3
- qkv_weight: bfloat16 [3, 1152, 1152], P(None, 'mp'), may hold values from -0.1875 to 0.1875
- qv_bias: bfloat16 [2, 1152], P(None, 'mp'), may hold values from -3 to 3
- out_weight: bfloat16 [1152, 1152], P('mp'), may hold values from -1.75 to 1.75
- out_bias: bfloat16 [1152], replicated, may hold values from -3 to 3
- up_weight: bfloat16 [4608, 1152], P('mp'), may hold values from -0.1875 to 0.1875
- up_bias: bfloat16 [4608], P('mp'), may hold values from -3 to 3
- down_weight: bfloat16 [4608, 1152], P('mp'), may hold values from -0.1875 to 0.1875
- down_bias: bfloat16 [1152], replicated, may hold values from -3 to 3
Outputs:
- layer_out: bfloat16 [8192, 1152], P(('dp', 'mp'))
- tokens_grad: bfloat16 [8192, 1152], P(('dp', 'mp'))
- ada_weight_grad: float32 [6912, 1152], P(('dp', 'mp'))
- ada_bias_grad: float32 [6912], P(('dp', 'mp'))
- qkv_weight_grad: float32 [3, 1152, 1152], P(None, 'mp')
- qv_bias_grad: float32 [2, 1152], P(None, 'mp')
- out_weight_grad: float32 [1152, 1152], P('mp')
- out_bias_grad: float32 [1152], replicated
- up_weight_grad: float32 [4608, 1152], P('mp')
- up_bias_grad: float32 [4608], P('mp')
- down_weight_grad: float32 [4608, 1152], P('mp')
- down_bias_grad: float32 [1152], replicated
The draws below stay inside these ranges and needn't reach their ends.
Inputs may be any that keep to these rules, and one draw needn't show every extreme that they name: `routes`: each row is a permutation of the image's 256 token positions. An image keeps the first keep_count of its routed slots; some image keeps exactly 192.
All inputs are finite; a program needn't handle non-finite values.
Results may differ from the reference program's by a relative error of at most 0.02.
The reference program's roundings to bfloat16 on the way count: a program that leaves them out, or rounds other values in their place, can miss the bound.
Values may be sent and summed in bfloat16 or wider, within the bound.
No kernel may reach another device: no remote copies, remote signals or barrier semaphores. Data moves between devices by JAX's collectives and lax.ppermute only.
A program may use at most 192 MiB of HBM per device.

```python
import math
import jax
import jax.numpy as jnp
from jax import lax

D = 1152
HEADS = 16
FF = 4608
P_SIZE = 256
CAP = 192
KEEP_MIN = 64
IMAGES = 32
TOKENS = 8192


def draw_keep_count(key, part):
    first, second, third = jax.random.split(key, 3)
    counts = jax.random.randint(first, (IMAGES,), KEEP_MIN, CAP + 1)
    fullest = jax.random.randint(second, (), 0, IMAGES)
    emptiest = (fullest + 1 + jax.random.randint(third, (), 0, IMAGES - 1)) % IMAGES
    counts = counts.at[fullest].set(CAP)
    return counts.at[emptiest].set(KEEP_MIN).astype(jnp.int32)


def shard_levels(rng, shape, cuts, smallest, largest):
    level = 1.0
    for axis_at, shards_of in cuts:
        steps = jax.random.uniform(jax.random.fold_in(jax.random.fold_in(rng, 6), axis_at), (shards_of,), jnp.float32, smallest / len(cuts), largest / len(cuts))
        level = level * jnp.repeat(jnp.exp(steps), shape[axis_at] // shards_of).reshape((-1,) + (1,) * (len(shape) - 1 - axis_at))
    return level


def bell_draw(rng, extent, width, limit, pieces=(), dtype=jnp.bfloat16):
    entries = jax.random.normal(rng, extent, jnp.float32) * width
    if len(pieces) > 0:
        entries = shard_levels(rng, extent, pieces, -0.22, 0.18) * entries
    return jnp.clip(entries, min=-limit, max=limit).astype(dtype)


def setup_inputs(seed: int = 0) -> dict:
    streams_of = jax.random.split(jax.random.key(seed), 16)
    return {
        "tokens": bell_draw(streams_of[0], (TOKENS, D), 1.0, 6.0, ((0, 32),)),
        "conditioning": bell_draw(streams_of[1], (IMAGES, D), 1.0, 6.0, ((0, 32),)),
        "routes": jax.vmap(lambda own: jax.random.permutation(own, P_SIZE))(jax.random.split(streams_of[2], IMAGES)).reshape((IMAGES, P_SIZE)).astype(jnp.int32),
        "keep_count": draw_keep_count(jax.random.fold_in(streams_of[15], 71), 0),
        "cotangent": bell_draw(streams_of[4], (TOKENS, D), 1.0, 6.0, ((0, 32),)),
        "ada_weight": bell_draw(streams_of[5], (6 * D, D), D ** -0.5, 0.1875),
        "ada_bias": bell_draw(streams_of[6], (6 * D,), 0.5, 3.0),
        "qkv_weight": bell_draw(streams_of[7], (3, D, D), D ** -0.5, 0.1875, ((1, 4),)),
        "qv_bias": bell_draw(streams_of[8], (2, D), 0.5, 3.0, ((1, 4),)),
        "out_weight": bell_draw(streams_of[9], (D, D), (D // 96) ** -0.5, 1.75, ((0, 4),)),
        "out_bias": bell_draw(streams_of[10], (D,), 0.4, 3.0),
        "up_weight": bell_draw(streams_of[11], (FF, D), D ** -0.5, 0.1875, ((0, 4),)),
        "up_bias": bell_draw(streams_of[12], (FF,), 0.5, 3.0, ((0, 4),)),
        "down_weight": bell_draw(streams_of[13], (FF, D), (FF // 4) ** -0.5, 0.1875, ((0, 4),)),
        "down_bias": bell_draw(streams_of[14], (D,), 0.4, 3.0),
    }


@jax.custom_vjp
def low(v):
    return lax.optimization_barrier(v.astype(jnp.bfloat16)).astype(jnp.float32)

@jax.custom_vjp
def low_back(v):
    return v

def low_keep(v):
    return (low(v), None)

def low_pass(kept, grad):
    return (grad,)

def back_keep(v):
    return (v, None)

def back_low(kept, grad):
    return (low(grad),)
low.defvjp(low_keep, low_pass)
low_back.defvjp(back_keep, back_low)
EPS = 1e-06

def exact_dot(left, right):
    return jnp.dot(left, right, precision=lax.Precision.HIGHEST, preferred_element_type=jnp.float32)

def both_ways(value):
    return low_back(low(value))

def layer_norm(rows):
    mean = lax.optimization_barrier(jnp.mean(rows, axis=-1, keepdims=True))
    centred = rows - mean
    return centred * lax.rsqrt(lax.optimization_barrier(jnp.mean(centred * centred, axis=-1, keepdims=True)) + EPS)

def place_rows(base, spots, rows):
    return base.at[spots].set(rows)

def image_block(params, image_rows, cond_rows, route_rows, keep_rows):
    ada_weight, ada_bias, qkv_weight, qv_bias, out_weight, out_bias, up_weight, up_bias, down_weight, down_bias = params
    batch = image_rows.shape[0]
    head_dim = D // HEADS
    score_scale = 1.0 / math.sqrt(head_dim)
    modulation = low_back(exact_dot(low(jax.nn.silu(cond_rows)), ada_weight.T) + ada_bias)
    blocks = [modulation[:, index * D:(index + 1) * D][:, None, :] for index in range(6)]
    shift_one, scale_one, gate_one, shift_two, scale_two, gate_two = blocks
    picks = route_rows[:, :CAP]
    routed = jnp.take_along_axis(image_rows, picks[:, :, None], axis=1)
    live_flat = (lax.broadcasted_iota(jnp.int32, (batch, CAP), 1) < keep_rows[:, None]).astype(jnp.float32)
    live = live_flat[:, :, None]
    mixed_one = low(layer_norm(routed) * (1.0 + scale_one) + shift_one).reshape(batch * CAP, D)
    query = both_ways(exact_dot(mixed_one, qkv_weight[0].T) + qv_bias[0]).reshape(batch, CAP, HEADS, head_dim)
    key = both_ways(exact_dot(mixed_one, qkv_weight[1].T)).reshape(batch, CAP, HEADS, head_dim)
    value = both_ways(exact_dot(mixed_one, qkv_weight[2].T) + qv_bias[1]).reshape(batch, CAP, HEADS, head_dim)
    scores = low_back(jnp.einsum('bthd,bshd->bhts', query, key, precision=lax.Precision.HIGHEST) * score_scale)
    scores = jnp.where(live_flat[:, None, None, :] > 0, scores, -1e+30)
    weights = low(jax.nn.softmax(scores, axis=-1))
    attended = both_ways(jnp.einsum('bhts,bshd->bthd', weights, value, precision=lax.Precision.HIGHEST)).reshape(batch * CAP, D)
    branch_one = low_back(exact_dot(attended, out_weight) + out_bias).reshape(batch, CAP, D)
    hidden_one = routed + live * gate_one * branch_one
    mixed_two = low(layer_norm(hidden_one) * (1.0 + scale_two) + shift_two).reshape(batch * CAP, D)
    before = low_back(exact_dot(mixed_two, up_weight.T) + up_bias)
    active = low(jax.nn.gelu(before, approximate=True))
    branch_two = low_back(exact_dot(active, down_weight) + down_bias).reshape(batch, CAP, D)
    hidden_two = hidden_one + live * gate_two * branch_two
    return jax.vmap(place_rows)(image_rows, picks, hidden_two)

def reference(tokens, conditioning, routes, keep_count, cotangent, ada_weight, ada_bias, qkv_weight, qv_bias, out_weight, out_bias, up_weight, up_bias, down_weight, down_bias):
    step_images = math.gcd(IMAGES, 16)
    turns = IMAGES // step_images
    image_rows = tokens.astype(jnp.float32).reshape(turns, step_images, P_SIZE, D)
    cond_rows = conditioning.astype(jnp.float32).reshape(turns, step_images, D)
    route_rows = routes.reshape(turns, step_images, P_SIZE)
    keep_rows = keep_count.reshape(turns, step_images)
    params = tuple((weight_arg.astype(jnp.float32) for weight_arg in (ada_weight, ada_bias, qkv_weight, qv_bias, out_weight, out_bias, up_weight, up_bias, down_weight, down_bias)))
    block = jax.checkpoint(image_block)

    def forward(params, image_rows):

        def advance(carry, items):
            rows, cond_part, route_part, keep_part = items
            return (carry, block(params, rows, cond_part, route_part, keep_part))
        _, outputs = lax.scan(advance, jnp.zeros((), jnp.float32), (image_rows, cond_rows, route_rows, keep_rows))
        return outputs
    layer_out, pull = jax.vjp(forward, params, image_rows)
    param_grads, token_grads = pull(cotangent.astype(jnp.float32).reshape(turns, step_images, P_SIZE, D))
    return (layer_out.reshape(TOKENS, D).astype(jnp.bfloat16), token_grads.reshape(TOKENS, D).astype(jnp.bfloat16), param_grads[0], param_grads[1], param_grads[2], param_grads[3], param_grads[4], param_grads[5], param_grads[6], param_grads[7], param_grads[8], param_grads[9])
```

```python
import functools
import math

import jax
import jax.numpy as jnp
from jax import lax
from jax.experimental import pallas as pl
from jax.experimental.pallas import tpu as pltpu
from jax.sharding import PartitionSpec as P

HEADS = 16
EPS = 1e-06
F32 = jnp.float32
BF16 = jnp.bfloat16
GELU_A = math.sqrt(2.0 / math.pi)
GELU_B = 0.044715


def norm_rows(rows):
    mean = jnp.mean(rows, axis=-1, keepdims=True)
    centred = rows - mean
    rstd = lax.rsqrt(jnp.mean(centred * centred, axis=-1, keepdims=True) + EPS)
    return centred * rstd, rstd


def norm_back(normed, rstd, grad):
    return rstd * (
        grad
        - jnp.mean(grad, axis=-1, keepdims=True)
        - normed * jnp.mean(grad * normed, axis=-1, keepdims=True)
    )


def mm(left, right, dims=((1,), (0,))):
    return lax.dot_general(left, right, (dims, ((), ())), preferred_element_type=F32)


NT = ((1,), (1,))
TN = ((0,), (0,))


def block(shape):
    rank = len(shape)
    return pl.BlockSpec((1,) + tuple(shape[1:]), lambda i: (i,) + (0,) * (rank - 1))


def whole(shape):
    rank = len(shape)
    return pl.BlockSpec(tuple(shape), lambda i: (0,) * rank)


def call(body, name, grid, ins, outs):
    return pl.pallas_call(
        body,
        grid=(grid,),
        in_specs=[block(a.shape) if step else whole(a.shape) for a, step in ins],
        out_specs=[block(shape) for shape, _ in outs],
        out_shape=[jax.ShapeDtypeStruct(shape, dtype) for shape, dtype in outs],
        name=name,
    )(*[a for a, _ in ins])


def gather_body(picks, tokens, cotangent, routed, grad_two):
    slots, patches = routed.shape[1], tokens.shape[1]
    hot = (lax.broadcasted_iota(jnp.int32, (slots, patches), 1) == picks[0]).astype(F32)
    hot = hot.astype(BF16)
    routed[0] = mm(hot, tokens[0]).astype(BF16)
    grad_two[0] = mm(hot, cotangent[0]).astype(BF16)


def mod_row(mod, index):
    return mod[0][index : index + 1, :]


def live_rows(keep, slots):
    return (lax.broadcasted_iota(jnp.int32, (slots, 1), 0).astype(F32) < keep[0][:, :1]).astype(F32)


def live_keys(keep, slots):
    return lax.broadcasted_iota(jnp.int32, (1, slots), 1).astype(F32) < keep[0][:, :1]


def head_mask(head, head_dim, cols):
    lane = lax.broadcasted_iota(jnp.int32, (1, cols), 1)
    inside = jnp.logical_and(lane >= head * head_dim, lane < (head + 1) * head_dim)
    return inside.astype(F32).astype(BF16)


def softmax_of(query, key, alive, scale):
    scores = mm(query, key, NT) * scale
    scores = jnp.where(alive, scores, -1e30)
    raised = jnp.exp(scores - jnp.max(scores, axis=-1, keepdims=True))
    return raised / jnp.sum(raised, axis=-1, keepdims=True)


def attend_body(head_dim, routed, mod, keep, weight, bias, out_weight, mixed, qkv, attended, branch):
    slots, cols = routed.shape[1], weight.shape[1]
    scale = 1.0 / math.sqrt(head_dim)
    normed, _ = norm_rows(routed[0].astype(F32))
    rows = (normed * (1.0 + mod_row(mod, 1)) + mod_row(mod, 0)).astype(BF16)
    mixed[0] = rows
    query = (mm(rows, weight[0], NT) + bias[0:1, :]).astype(BF16)
    key = mm(rows, weight[1], NT).astype(BF16)
    value = (mm(rows, weight[2], NT) + bias[1:2, :]).astype(BF16)
    qkv[0, 0] = query
    qkv[0, 1] = key
    qkv[0, 2] = value
    alive = live_keys(keep, slots)
    total = jnp.zeros((slots, cols), F32)
    for head in range(cols // head_dim):
        mask = head_mask(head, head_dim, cols)
        low = softmax_of(query * mask, key, alive, scale).astype(BF16)
        total = total + mm(low, value * mask)
    total = total.astype(BF16)
    attended[0] = total
    branch[0] = mm(total, out_weight[...]).astype(BF16)


def attend_back_body(
    head_dim, grad, qkv, routed, keep, weight, out_weight, qkv_grad, mixed_grad, stats, bias_sums
):
    slots, cols = routed.shape[1], weight.shape[1]
    scale = 1.0 / math.sqrt(head_dim)
    rows_grad = grad[0]
    attended_grad = mm(rows_grad, out_weight[...], NT).astype(BF16)
    query, key, value = qkv[0, 0], qkv[0, 1], qkv[0, 2]
    alive = live_keys(keep, slots)
    query_grad = jnp.zeros((slots, cols), F32)
    key_grad = jnp.zeros((slots, cols), F32)
    value_grad = jnp.zeros((slots, cols), F32)
    for head in range(cols // head_dim):
        mask = head_mask(head, head_dim, cols)
        own_query = query * mask
        weights = softmax_of(own_query, key, alive, scale)
        own_grad = attended_grad * mask
        weight_grad = mm(own_grad, value, NT)
        value_grad = value_grad + mm(weights.astype(BF16), own_grad, TN)
        row_total = jnp.sum(weights * weight_grad, axis=-1, keepdims=True)
        score_grad = (weights * (weight_grad - row_total)).astype(BF16)
        query_grad = query_grad + mm(score_grad, key * mask)
        key_grad = key_grad + mm(score_grad, own_query, TN)
    query_grad = (query_grad * scale).astype(BF16)
    key_grad = (key_grad * scale).astype(BF16)
    value_grad = value_grad.astype(BF16)
    qkv_grad[0, 0] = query_grad
    qkv_grad[0, 1] = key_grad
    qkv_grad[0, 2] = value_grad
    rows = mm(query_grad, weight[0]) + mm(key_grad, weight[1]) + mm(value_grad, weight[2])
    mixed_grad[0] = rows.astype(BF16)
    normed, _ = norm_rows(routed[0].astype(F32))
    stats[0, 0:1, :] = jnp.sum(rows, axis=0, keepdims=True)
    stats[0, 1:2, :] = jnp.sum(rows * normed, axis=0, keepdims=True)
    stats[0, 2:3, :] = jnp.sum(rows_grad.astype(F32), axis=0, keepdims=True)
    bias_sums[0, 0:1, :] = jnp.sum(query_grad.astype(F32), axis=0, keepdims=True)
    bias_sums[0, 1:2, :] = jnp.sum(value_grad.astype(F32), axis=0, keepdims=True)


def forward_body(
    mixed, grad_two, mod, keep, up, up_bias, down,
    active, before_grad, down_grad, branch, mixed_grad, up_sum, down_sum,
):
    slots = mixed.shape[1]
    gate = live_rows(keep, slots) * mod_row(mod, 5)
    rows_grad = (gate * grad_two[0].astype(F32)).astype(BF16)
    down_grad[0] = rows_grad
    down_sum[0] = jnp.sum(rows_grad.astype(F32), axis=0, keepdims=True)
    before = mm(mixed[0], up[...], NT) + up_bias[...]
    square = before * before
    tanh = jnp.tanh(GELU_A * (before + GELU_B * (before * square)))
    half = 0.5 * (1.0 + tanh)
    act = (before * half).astype(BF16)
    active[0] = act
    slope = half + 0.5 * before * (1.0 - tanh * tanh) * (GELU_A * (1.0 + 3.0 * GELU_B * square))
    inner = (mm(rows_grad, down[...], NT) * slope).astype(BF16)
    before_grad[0] = inner
    up_sum[0] = jnp.sum(inner.astype(F32), axis=0, keepdims=True)
    mixed_grad[0] = mm(inner, up[...]).astype(BF16)
    branch[0] = mm(act, down[...]).astype(BF16)


def middle_body(branch, out_bias, routed, mod, keep, hidden, mixed):
    slots = routed.shape[1]
    branch_one = branch[0].astype(F32) + out_bias[...]
    rows = routed[0].astype(F32) + live_rows(keep, slots) * mod_row(mod, 2) * branch_one
    hidden[0] = rows
    normed, _ = norm_rows(rows)
    mixed[0] = (normed * (1.0 + mod_row(mod, 4)) + mod_row(mod, 3)).astype(BF16)


def middle_back_body(
    mixed_grad, hidden, branch, out_bias, grad_two, mod, keep, grad_one, branch_grad, stats
):
    slots = hidden.shape[1]
    rows = mixed_grad[0].astype(F32)
    normed, rstd = norm_rows(hidden[0])
    grad = grad_two[0].astype(F32) + norm_back(normed, rstd, rows * (1.0 + mod_row(mod, 4)))
    grad_one[0] = grad
    live = live_rows(keep, slots)
    branch_one = branch[0].astype(F32) + out_bias[...]
    stats[0, 0:1, :] = jnp.sum(live * grad * branch_one, axis=0, keepdims=True)
    stats[0, 1:2, :] = jnp.sum(rows, axis=0, keepdims=True)
    stats[0, 2:3, :] = jnp.sum(rows * normed, axis=0, keepdims=True)
    branch_grad[0] = (live * mod_row(mod, 2) * grad).astype(BF16)


def place(picks, base, rows):
    patches, slots = base.shape[0], rows.shape[0]
    hot = (lax.broadcasted_iota(jnp.int32, (patches, slots), 0) == picks).astype(F32)
    taken = jnp.max(hot, axis=1, keepdims=True) > 0
    return jnp.where(taken, mm(hot.astype(BF16), rows.astype(BF16)), base.astype(F32)).astype(BF16)


def out_body(branch, hidden, down_bias, mod, keep, grad_two, picks, tokens, layer_out, gate_grad):
    slots = hidden.shape[1]
    live = live_rows(keep, slots)
    branch_two = branch[0].astype(F32) + down_bias[...]
    gate_grad[0] = jnp.sum(live * grad_two[0].astype(F32) * branch_two, axis=0, keepdims=True)
    rows = hidden[0] + live * mod_row(mod, 5) * branch_two
    layer_out[0] = place(picks[0], tokens[0], rows)


def first_back_body(mixed_grad, routed, mod, grad_one, picks, cotangent, tokens_grad):
    normed, rstd = norm_rows(routed[0].astype(F32))
    rows = mixed_grad[0].astype(F32) * (1.0 + mod_row(mod, 1))
    tokens_grad[0] = place(picks[0], cotangent[0], grad_one[0] + norm_back(normed, rstd, rows))


def dp_bits():
    count = lax.axis_size("dp").bit_length() - 1
    return list(range(count))


def partner(bit):
    return [(i, i ^ (1 << bit)) for i in range(lax.axis_size("dp"))]


def scatter_sum(part, bits):
    index = lax.axis_index("dp")
    for bit in bits:
        side = (index >> bit) & 1
        halves = part.reshape(2, part.shape[0] // 2, part.shape[1])
        own = lax.dynamic_index_in_dim(halves, side, 0, keepdims=False)
        other = lax.dynamic_index_in_dim(halves, 1 - side, 0, keepdims=False)
        got = lax.ppermute(other, "dp", partner(bit))
        part = (own.astype(F32) + got.astype(F32)).astype(BF16)
    return part


def gather_rows(part, bits):
    index = lax.axis_index("dp")
    for bit in reversed(bits):
        side = (index >> bit) & 1
        got = lax.ppermute(part, "dp", partner(bit))
        part = jnp.where(
            side == 0, jnp.concatenate([part, got], 0), jnp.concatenate([got, part], 0)
        )
    return part


def shift(value, step):
    count = lax.axis_size("mp")
    return lax.ppermute(value, "mp", [(i, (i + step) % count) for i in range(count)])


def small_gather(value):
    count, here = lax.axis_size("mp"), lax.axis_index("mp")
    rows = jnp.stack([value] + [shift(value, step) for step in range(1, count)])
    return jnp.take(rows, (here - jnp.arange(count)) % count, axis=0)


def small_scatter_sum(parts):
    count, here = lax.axis_size("mp"), lax.axis_index("mp")
    total = lax.dynamic_index_in_dim(parts, here, 0, keepdims=False)
    for step in range(1, count):
        to = (here + step) % count
        total = total + shift(lax.dynamic_index_in_dim(parts, to, 0, keepdims=False), step)
    return total


def sum_pair(first, second):
    bits = dp_bits()
    turned = bits[:1] + bits[2:] + bits[1:2]
    first = scatter_sum(first, bits)
    second = scatter_sum(second, turned)
    return gather_rows(first, bits), gather_rows(second, turned)


def per_device(
    tokens, conditioning, routes, keep_count, cotangent, ada_weight, ada_bias, qkv_weight,
    qv_bias, out_weight, out_bias, up_weight, up_bias, down_weight, down_bias,
):
    images = conditioning.shape[0]
    width = tokens.shape[1]
    patches = routes.shape[1]
    slots = 3 * patches // 4
    cols = qkv_weight.shape[1]
    head_dim = width // HEADS
    hidden_units = up_weight.shape[0]
    members = lax.axis_size("mp")
    groups = lax.axis_size("dp")
    group = members * images
    here = lax.axis_index("mp")

    image_tokens = tokens.reshape(images, patches, width)
    image_cot = cotangent.reshape(images, patches, width)
    picks = routes[:, :slots]
    picks_col = picks.reshape(images, slots, 1)
    picks_row = picks.reshape(images, 1, slots)
    rows_shape = (images, slots, width)
    group_shape = (group, slots, width)

    routed, grad_two = call(
        gather_body, "gather", images,
        [(picks_col, True), (image_tokens, True), (image_cot, True)],
        [(rows_shape, BF16), (rows_shape, BF16)],
    )
    group_routed = lax.all_gather(routed, "mp", axis=0, tiled=True)
    group_two = lax.all_gather(grad_two, "mp", axis=0, tiled=True)

    small = jnp.concatenate(
        [conditioning, jnp.broadcast_to(keep_count.astype(BF16)[:, None], (images, 128))], axis=1
    )
    small = small_gather(small).reshape(group, width + 128)
    silu_cond = jax.nn.silu(small[:, :width].astype(F32)).astype(BF16)
    modulation = mm(silu_cond, ada_weight, NT) + ada_bias.astype(F32)
    modulation = modulation.reshape(group, 6, width)
    keep = small[:, None, width:].astype(F32)
    own_mod = lax.dynamic_slice_in_dim(modulation, here * images, images, 0)
    own_keep = jnp.broadcast_to(keep_count.astype(F32)[:, None, None], (images, 1, 128))
    out_bias_row = out_bias.astype(F32)[None]
    down_bias_row = down_bias.astype(F32)[None]

    mixed_one, qkv, attended, branch = call(
        functools.partial(attend_body, head_dim), "attend", group,
        [
            (group_routed, True), (modulation, True), (keep, True), (qkv_weight, False),
            (qv_bias.astype(F32), False), (out_weight, False),
        ],
        [
            (group_shape, BF16), ((group, 3, slots, cols), BF16), ((group, slots, cols), BF16),
            (group_shape, BF16),
        ],
    )
    branch_one = lax.psum_scatter(branch, "mp", scatter_dimension=0, tiled=True)
    hidden_one, mixed_two = call(
        middle_body, "middle", images,
        [
            (branch_one, True), (out_bias_row, False), (routed, True), (own_mod, True),
            (own_keep, True),
        ],
        [(rows_shape, F32), (rows_shape, BF16)],
    )
    group_mixed = lax.all_gather(mixed_two, "mp", axis=0, tiled=True)
    unit_shape = (group, slots, hidden_units)
    active, before_grad, down_grad, branch, mixed_grad, up_sum, down_sum = call(
        forward_body, "forward", group,
        [
            (group_mixed, True), (group_two, True), (modulation, True), (keep, True),
            (up_weight, False), (up_bias.astype(F32)[None], False), (down_weight, False),
        ],
        [
            (unit_shape, BF16), (unit_shape, BF16), (group_shape, BF16), (group_shape, BF16),
            (group_shape, BF16), ((group, 1, hidden_units), F32), ((group, 1, width), F32),
        ],
    )
    mixed_two_grad = lax.psum_scatter(mixed_grad, "mp", scatter_dimension=0, tiled=True)
    branch_two = lax.psum_scatter(branch, "mp", scatter_dimension=0, tiled=True)

    flat = (group * slots, hidden_units)
    wide = (group * slots, width)
    up_part = mm(before_grad.reshape(flat), group_mixed.reshape(wide), TN).astype(BF16)
    down_part = mm(active.reshape(flat), down_grad.reshape(wide), TN).astype(BF16)
    up_weight_grad, down_weight_grad = sum_pair(up_part, down_part)

    grad_one, branch_grad, middle_stats = call(
        middle_back_body, "middle_back", images,
        [
            (mixed_two_grad, True), (hidden_one, True), (branch_one, True), (out_bias_row, False),
            (grad_two, True), (own_mod, True), (own_keep, True),
        ],
        [(rows_shape, F32), (rows_shape, BF16), ((images, 3, width), F32)],
    )
    group_grad = lax.all_gather(branch_grad, "mp", axis=0, tiled=True)
    layer_out, gate_grad = call(
        out_body, "out", images,
        [
            (branch_two, True), (hidden_one, True), (down_bias_row, False), (own_mod, True),
            (own_keep, True), (grad_two, True), (picks_row, True), (image_tokens, True),
        ],
        [((images, patches, width), BF16), ((images, 1, width), F32)],
    )
    qkv_grad, mixed_grad, attend_stats, bias_sums = call(
        functools.partial(attend_back_body, head_dim), "attend_back", group,
        [
            (group_grad, True), (qkv, True), (group_routed, True), (keep, True),
            (qkv_weight, False), (out_weight, False),
        ],
        [
            ((group, 3, slots, cols), BF16), (group_shape, BF16), ((group, 3, width), F32),
            ((group, 2, cols), F32),
        ],
    )
    mixed_one_grad = lax.psum_scatter(mixed_grad, "mp", scatter_dimension=0, tiled=True)

    qkv_part = jnp.einsum(
        "gtsc,gsd->tcd", qkv_grad, mixed_one, preferred_element_type=F32
    ).reshape(3 * cols, width)
    out_part = mm(attended.reshape(-1, cols), group_grad.reshape(wide), TN)
    part = jnp.concatenate([qkv_part.astype(BF16), out_part.astype(BF16)], axis=0)
    part = jnp.concatenate(sum_pair(part[: 2 * cols], part[2 * cols :]), axis=0)
    qkv_weight_grad = part[: 3 * cols].reshape(3, cols, width)
    out_weight_grad = part[3 * cols :]

    own_rows = jnp.concatenate([middle_stats, gate_grad], axis=1)
    placed = lax.dynamic_update_slice(
        jnp.zeros((group, 4, width), F32), own_rows, (here * images, 0, 0)
    )
    mod_grad = jnp.concatenate([attend_stats[:, :2], placed], axis=1)
    each = 6 * width // (groups * members)
    mod_grad = mod_grad.reshape(group, groups, members, each)
    mod_grad = small_scatter_sum(mod_grad.transpose(2, 0, 1, 3)).astype(BF16)
    pieces = [
        mod_grad.reshape(-1),
        silu_cond.reshape(-1),
        jnp.sum(bias_sums, axis=0).astype(BF16).reshape(-1),
        jnp.sum(attend_stats[:, 2], axis=0).astype(BF16),
        jnp.sum(up_sum, axis=0).astype(BF16).reshape(-1),
        jnp.sum(down_sum, axis=0).astype(BF16).reshape(-1),
    ]
    sizes = [piece.shape[0] for piece in pieces]
    packed = jnp.concatenate(pieces)
    packed = jnp.pad(packed, (0, -packed.shape[0] % 2048)).reshape(-1, 128)
    packed = lax.all_gather(packed, "dp", axis=0, tiled=False).reshape(groups, -1)
    starts = [sum(sizes[:i]) for i in range(len(sizes))]
    views = [packed[:, s : s + n] for s, n in zip(starts, sizes)]
    mod_all = views[0].reshape(groups, group, groups, each)
    mod_all = lax.dynamic_index_in_dim(mod_all, lax.axis_index("dp"), 2, keepdims=False)
    mod_all = mod_all.reshape(groups * group, each)
    cond_all = views[1].reshape(groups * group, width)
    ada_weight_grad = mm(mod_all, cond_all, TN)
    ada_bias_grad = jnp.sum(mod_all.astype(F32), axis=0)
    qv_sum, out_sum, up_bias_grad, down_bias_grad = [
        jnp.sum(view.astype(F32), axis=0) for view in views[2:]
    ]

    tokens_grad = call(
        first_back_body, "first_back", images,
        [
            (mixed_one_grad, True), (routed, True), (own_mod, True), (grad_one, True),
            (picks_row, True), (image_cot, True),
        ],
        [((images, patches, width), BF16)],
    )[0]
    return (
        layer_out.reshape(images * patches, width),
        tokens_grad.reshape(images * patches, width),
        ada_weight_grad,
        ada_bias_grad,
        qkv_weight_grad.astype(F32),
        qv_sum.reshape(2, cols),
        out_weight_grad.astype(F32),
        out_sum,
        up_weight_grad.astype(F32),
        up_bias_grad,
        down_weight_grad.astype(F32),
        down_bias_grad,
    )


def solution(mesh):
    both = ("dp", "mp")
    in_specs = (
        P(both, None), P(both, None), P(both, None), P(both), P(both, None), P(), P(),
        P(None, "mp", None), P(None, "mp"), P("mp", None), P(), P("mp", None), P("mp"),
        P("mp", None), P(),
    )
    out_specs = (
        P(both, None), P(both, None), P(both, None), P(both), P(None, "mp", None), P(None, "mp"),
        P("mp", None), P(), P("mp", None), P("mp"), P("mp", None), P(),
    )
    return jax.shard_map(
        per_device, mesh=mesh, in_specs=in_specs, out_specs=out_specs, check_vma=False
    )
```

```python
import functools
import math

import jax
import jax.numpy as jnp
from jax import lax
from jax.experimental import pallas as pl
from jax.sharding import PartitionSpec as P


HEADS = 16
EPS = 1e-06
F32 = jnp.float32
BF16 = jnp.bfloat16
GELU_A = math.sqrt(2.0 / math.pi)
GELU_B = 0.044715


def norm_rows(rows):
    mean = jnp.mean(rows, axis=-1, keepdims=True)
    centred = rows - mean
    rstd = lax.rsqrt(jnp.mean(centred * centred, axis=-1, keepdims=True) + EPS)
    return centred * rstd, rstd


def norm_back(normed, rstd, grad):
    return rstd * (
        grad
        - jnp.mean(grad, axis=-1, keepdims=True)
        - normed * jnp.mean(grad * normed, axis=-1, keepdims=True)
    )


def mm(left, right, dims=((1,), (0,))):
    return lax.dot_general(left, right, (dims, ((), ())), preferred_element_type=F32)


NT = ((1,), (1,))
TN = ((0,), (0,))


def block(shape):
    rank = len(shape)
    return pl.BlockSpec((1,) + tuple(shape[1:]), lambda i: (i,) + (0,) * (rank - 1))


def whole(shape):
    rank = len(shape)
    return pl.BlockSpec(tuple(shape), lambda i: (0,) * rank)


def call(body, grid, ins, outs):
    return pl.pallas_call(
        body,
        grid=(grid,),
        in_specs=[block(a.shape) if step else whole(a.shape) for a, step in ins],
        out_specs=[block(shape) for shape, _ in outs],
        out_shape=[jax.ShapeDtypeStruct(shape, dtype) for shape, dtype in outs],
    )(*[a for a, _ in ins])


def gather_body(picks, tokens, cotangent, routed, grad_two):
    slots, patches = routed.shape[1], tokens.shape[1]
    hot = (lax.broadcasted_iota(jnp.int32, (slots, patches), 1) == picks[0]).astype(F32)
    hot = hot.astype(BF16)
    routed[0] = mm(hot, tokens[0]).astype(BF16)
    grad_two[0] = mm(hot, cotangent[0]).astype(BF16)


def mod_row(mod, index):
    return mod[0][index : index + 1, :]


def live_rows(keep, slots):
    return (lax.broadcasted_iota(jnp.int32, (slots, 1), 0).astype(F32) < keep[0][:, :1]).astype(F32)


def live_keys(keep, slots):
    return lax.broadcasted_iota(jnp.int32, (1, slots), 1).astype(F32) < keep[0][:, :1]


def head_mask(head, head_dim, cols):
    lane = lax.broadcasted_iota(jnp.int32, (1, cols), 1)
    inside = jnp.logical_and(lane >= head * head_dim, lane < (head + 1) * head_dim)
    return inside.astype(F32).astype(BF16)


def softmax_of(query, key, alive, scale):
    scores = mm(query, key, NT) * scale
    scores = jnp.where(alive, scores, -1e30)
    raised = jnp.exp(scores - jnp.max(scores, axis=-1, keepdims=True))
    return raised / jnp.sum(raised, axis=-1, keepdims=True)


def attend_body(head_dim, routed, mod, keep, weight, bias, out_weight, mixed, qkv, attended, branch):
    slots, cols = routed.shape[1], weight.shape[1]
    scale = 1.0 / math.sqrt(head_dim)
    normed, _ = norm_rows(routed[0].astype(F32))
    rows = (normed * (1.0 + mod_row(mod, 1)) + mod_row(mod, 0)).astype(BF16)
    mixed[0] = rows
    query = (mm(rows, weight[0], NT) + bias[0:1, :]).astype(BF16)
    key = mm(rows, weight[1], NT).astype(BF16)
    value = (mm(rows, weight[2], NT) + bias[1:2, :]).astype(BF16)
    qkv[0, 0] = query
    qkv[0, 1] = key
    qkv[0, 2] = value
    alive = live_keys(keep, slots)
    total = jnp.zeros((slots, cols), F32)
    for head in range(cols // head_dim):
        mask = head_mask(head, head_dim, cols)
        low = softmax_of(query * mask, key, alive, scale).astype(BF16)
        total = total + mm(low, value * mask)
    total = total.astype(BF16)
    attended[0] = total
    branch[0] = mm(total, out_weight[...]).astype(BF16)


def attend_back_body(
    head_dim, grad, qkv, routed, keep, weight, out_weight, qkv_grad, mixed_grad, stats, bias_sums
):
    slots, cols = routed.shape[1], weight.shape[1]
    scale = 1.0 / math.sqrt(head_dim)
    rows_grad = grad[0]
    attended_grad = mm(rows_grad, out_weight[...], NT).astype(BF16)
    query, key, value = qkv[0, 0], qkv[0, 1], qkv[0, 2]
    alive = live_keys(keep, slots)
    query_grad = jnp.zeros((slots, cols), F32)
    key_grad = jnp.zeros((slots, cols), F32)
    value_grad = jnp.zeros((slots, cols), F32)
    for head in range(cols // head_dim):
        mask = head_mask(head, head_dim, cols)
        own_query = query * mask
        weights = softmax_of(own_query, key, alive, scale)
        own_grad = attended_grad * mask
        weight_grad = mm(own_grad, value, NT)
        value_grad = value_grad + mm(weights.astype(BF16), own_grad, TN)
        row_total = jnp.sum(weights * weight_grad, axis=-1, keepdims=True)
        score_grad = (weights * (weight_grad - row_total)).astype(BF16)
        query_grad = query_grad + mm(score_grad, key * mask)
        key_grad = key_grad + mm(score_grad, own_query, TN)
    query_grad = (query_grad * scale).astype(BF16)
    key_grad = (key_grad * scale).astype(BF16)
    value_grad = value_grad.astype(BF16)
    qkv_grad[0, 0] = query_grad
    qkv_grad[0, 1] = key_grad
    qkv_grad[0, 2] = value_grad
    rows = mm(query_grad, weight[0]) + mm(key_grad, weight[1]) + mm(value_grad, weight[2])
    mixed_grad[0] = rows.astype(BF16)
    normed, _ = norm_rows(routed[0].astype(F32))
    stats[0, 0:1, :] = jnp.sum(rows, axis=0, keepdims=True)
    stats[0, 1:2, :] = jnp.sum(rows * normed, axis=0, keepdims=True)
    stats[0, 2:3, :] = jnp.sum(rows_grad.astype(F32), axis=0, keepdims=True)
    bias_sums[0, 0:1, :] = jnp.sum(query_grad.astype(F32), axis=0, keepdims=True)
    bias_sums[0, 1:2, :] = jnp.sum(value_grad.astype(F32), axis=0, keepdims=True)


def forward_body(
    mixed, grad_two, mod, keep, up, up_bias, down,
    active, before_grad, down_grad, branch, mixed_grad, up_sum, down_sum,
):
    slots = mixed.shape[1]
    gate = live_rows(keep, slots) * mod_row(mod, 5)
    rows_grad = (gate * grad_two[0].astype(F32)).astype(BF16)
    down_grad[0] = rows_grad
    down_sum[0] = jnp.sum(rows_grad.astype(F32), axis=0, keepdims=True)
    before = mm(mixed[0], up[...], NT) + up_bias[...]
    square = before * before
    tanh = jnp.tanh(GELU_A * (before + GELU_B * (before * square)))
    half = 0.5 * (1.0 + tanh)
    act = (before * half).astype(BF16)
    active[0] = act
    slope = half + 0.5 * before * (1.0 - tanh * tanh) * (GELU_A * (1.0 + 3.0 * GELU_B * square))
    inner = (mm(rows_grad, down[...], NT) * slope).astype(BF16)
    before_grad[0] = inner
    up_sum[0] = jnp.sum(inner.astype(F32), axis=0, keepdims=True)
    mixed_grad[0] = mm(inner, up[...]).astype(BF16)
    branch[0] = mm(act, down[...]).astype(BF16)


def middle_body(branch, out_bias, routed, mod, keep, hidden, mixed):
    slots = routed.shape[1]
    branch_one = branch[0].astype(F32) + out_bias[...]
    rows = routed[0].astype(F32) + live_rows(keep, slots) * mod_row(mod, 2) * branch_one
    hidden[0] = rows
    normed, _ = norm_rows(rows)
    mixed[0] = (normed * (1.0 + mod_row(mod, 4)) + mod_row(mod, 3)).astype(BF16)


def middle_back_body(
    mixed_grad, hidden, branch, out_bias, grad_two, mod, keep, grad_one, branch_grad, stats
):
    slots = hidden.shape[1]
    rows = mixed_grad[0].astype(F32)
    normed, rstd = norm_rows(hidden[0])
    grad = grad_two[0].astype(F32) + norm_back(normed, rstd, rows * (1.0 + mod_row(mod, 4)))
    grad_one[0] = grad
    live = live_rows(keep, slots)
    branch_one = branch[0].astype(F32) + out_bias[...]
    stats[0, 0:1, :] = jnp.sum(live * grad * branch_one, axis=0, keepdims=True)
    stats[0, 1:2, :] = jnp.sum(rows, axis=0, keepdims=True)
    stats[0, 2:3, :] = jnp.sum(rows * normed, axis=0, keepdims=True)
    branch_grad[0] = (live * mod_row(mod, 2) * grad).astype(BF16)


def place(picks, base, rows):
    patches, slots = base.shape[0], rows.shape[0]
    hot = (lax.broadcasted_iota(jnp.int32, (patches, slots), 0) == picks).astype(F32)
    taken = jnp.max(hot, axis=1, keepdims=True) > 0
    return jnp.where(taken, mm(hot.astype(BF16), rows.astype(BF16)), base.astype(F32)).astype(BF16)


def out_body(branch, hidden, down_bias, mod, keep, grad_two, picks, tokens, layer_out, gate_grad):
    slots = hidden.shape[1]
    live = live_rows(keep, slots)
    branch_two = branch[0].astype(F32) + down_bias[...]
    gate_grad[0] = jnp.sum(live * grad_two[0].astype(F32) * branch_two, axis=0, keepdims=True)
    rows = hidden[0] + live * mod_row(mod, 5) * branch_two
    layer_out[0] = place(picks[0], tokens[0], rows)


def first_back_body(mixed_grad, routed, mod, grad_one, picks, cotangent, tokens_grad):
    normed, rstd = norm_rows(routed[0].astype(F32))
    rows = mixed_grad[0].astype(F32) * (1.0 + mod_row(mod, 1))
    tokens_grad[0] = place(picks[0], cotangent[0], grad_one[0] + norm_back(normed, rstd, rows))


def dp_bits():
    count = lax.axis_size("dp").bit_length() - 1
    return list(range(count))


def partner(bit):
    return [(i, i ^ (1 << bit)) for i in range(lax.axis_size("dp"))]


def halve(part, bit):
    side = (lax.axis_index("dp") >> bit) & 1
    halves = part.reshape(2, part.shape[0] // 2, part.shape[1])
    own = lax.dynamic_index_in_dim(halves, side, 0, keepdims=False)
    other = lax.dynamic_index_in_dim(halves, 1 - side, 0, keepdims=False)
    return own, lax.ppermute(other, "dp", partner(bit))


def add_low(own, got):
    return (own.astype(F32) + got.astype(F32)).astype(BF16)


def double(part, bit):
    return part, lax.ppermute(part, "dp", partner(bit))


def join(own, got, bit):
    side = (lax.axis_index("dp") >> bit) & 1
    return jnp.where(side == 0, jnp.concatenate([own, got], 0), jnp.concatenate([got, own], 0))


def after(value, *others):
    return lax.optimization_barrier((value,) + others)[0]


def orders():
    bits = dp_bits()
    return bits, bits[:1] + bits[2:] + bits[1:2]


def shift(value, step):
    count = lax.axis_size("mp")
    return lax.ppermute(value, "mp", [(i, (i + step) % count) for i in range(count)])


def small_gather(value):
    count, here = lax.axis_size("mp"), lax.axis_index("mp")
    rows = jnp.stack([value] + [shift(value, step) for step in range(1, count)])
    return jnp.take(rows, (here - jnp.arange(count)) % count, axis=0)


def small_scatter_sum(parts):
    count, here = lax.axis_size("mp"), lax.axis_index("mp")
    total = lax.dynamic_index_in_dim(parts, here, 0, keepdims=False)
    for step in range(1, count):
        to = (here + step) % count
        total = total + shift(lax.dynamic_index_in_dim(parts, to, 0, keepdims=False), step)
    return total


def sum_pair(parts):
    pairs = list(zip(parts, orders()))
    for level in range(len(dp_bits())):
        pairs = [(add_low(*halve(part, bits[level])), bits) for part, bits in pairs]
    for level in reversed(range(len(dp_bits()))):
        pairs = [(join(*double(part, bits[level]), bits[level]), bits) for part, bits in pairs]
    return [part for part, _ in pairs]


def all_rows(rows):
    return lax.all_gather(rows, "mp", axis=0, tiled=True)


def own_sum(rows):
    return lax.psum_scatter(rows, "mp", scatter_dimension=0, tiled=True)


def per_device(
    tokens, conditioning, routes, keep_count, cotangent, ada_weight, ada_bias, qkv_weight,
    qv_bias, out_weight, out_bias, up_weight, up_bias, down_weight, down_bias,
):
    images = conditioning.shape[0]
    width = tokens.shape[1]
    patches = routes.shape[1]
    slots = 3 * patches // 4
    cols = qkv_weight.shape[1]
    head_dim = width // HEADS
    hidden_units = up_weight.shape[0]
    members = lax.axis_size("mp")
    groups = lax.axis_size("dp")
    group = members * images
    here = lax.axis_index("mp")

    image_tokens = tokens.reshape(images, patches, width)
    image_cot = cotangent.reshape(images, patches, width)
    picks = routes[:, :slots]
    picks_col = picks.reshape(images, slots, 1)
    picks_row = picks.reshape(images, 1, slots)
    rows_shape = (images, slots, width)
    group_shape = (group, slots, width)

    routed, grad_two = call(
        gather_body, images,
        [(picks_col, True), (image_tokens, True), (image_cot, True)],
        [(rows_shape, BF16), (rows_shape, BF16)],
    )
    group_routed = all_rows(routed)
    group_two = all_rows(grad_two)

    small = jnp.concatenate(
        [conditioning, jnp.broadcast_to(keep_count.astype(BF16)[:, None], (images, 128))], axis=1
    )
    small = small_gather(small).reshape(group, width + 128)
    silu_cond = jax.nn.silu(small[:, :width].astype(F32)).astype(BF16)
    modulation = mm(silu_cond, ada_weight, NT) + ada_bias.astype(F32)
    modulation = modulation.reshape(group, 6, width)
    keep = small[:, None, width:].astype(F32)
    own_mod = lax.dynamic_slice_in_dim(modulation, here * images, images, 0)
    own_keep = jnp.broadcast_to(keep_count.astype(F32)[:, None, None], (images, 1, 128))
    out_bias_row = out_bias.astype(F32)[None]
    down_bias_row = down_bias.astype(F32)[None]

    mixed_one, qkv, attended, branch = call(
        functools.partial(attend_body, head_dim), group,
        [
            (group_routed, True), (modulation, True), (keep, True), (qkv_weight, False),
            (qv_bias.astype(F32), False), (out_weight, False),
        ],
        [
            (group_shape, BF16), ((group, 3, slots, cols), BF16), ((group, slots, cols), BF16),
            (group_shape, BF16),
        ],
    )
    branch_one = own_sum(branch)
    hidden_one, mixed_two = call(
        middle_body, images,
        [
            (branch_one, True), (out_bias_row, False), (routed, True), (own_mod, True),
            (own_keep, True),
        ],
        [(rows_shape, F32), (rows_shape, BF16)],
    )
    group_mixed = all_rows(mixed_two)
    unit_shape = (group, slots, hidden_units)
    active, before_grad, down_grad, branch, mixed_grad, up_sum, down_sum = call(
        forward_body, group,
        [
            (group_mixed, True), (group_two, True), (modulation, True), (keep, True),
            (up_weight, False), (up_bias.astype(F32)[None], False), (down_weight, False),
        ],
        [
            (unit_shape, BF16), (unit_shape, BF16), (group_shape, BF16), (group_shape, BF16),
            (group_shape, BF16), ((group, 1, hidden_units), F32), ((group, 1, width), F32),
        ],
    )
    mixed_two_grad = own_sum(mixed_grad)

    flat = (group * slots, hidden_units)
    wide = (group * slots, width)
    up_part = mm(before_grad.reshape(flat), group_mixed.reshape(wide), TN).astype(BF16)
    down_part = mm(active.reshape(flat), down_grad.reshape(wide), TN).astype(BF16)
    levels = len(dp_bits())
    ways = orders()
    sums = [add_low(*halve(part, way[0])) for part, way in zip((up_part, down_part), ways)]
    flights = [halve(part, way[1]) for part, way in zip(sums, ways)]

    grad_one, branch_grad, middle_stats = call(
        middle_back_body, images,
        [
            (mixed_two_grad, True), (hidden_one, True), (branch_one, True), (out_bias_row, False),
            (grad_two, True), (own_mod, True), (own_keep, True),
        ],
        [(rows_shape, F32), (rows_shape, BF16), ((images, 3, width), F32)],
    )
    group_grad = all_rows(branch_grad)
    sums = [add_low(after(own, branch_grad), got) for own, got in flights]
    for level in range(2, levels):
        sums = [add_low(*halve(part, way[level])) for part, way in zip(sums, ways)]
    for level in reversed(range(2, levels)):
        sums = [join(*double(part, way[level]), way[level]) for part, way in zip(sums, ways)]
    flights = [double(part, way[1]) for part, way in zip(sums, ways)]
    branch_two = own_sum(branch)
    layer_out, gate_grad = call(
        out_body, images,
        [
            (branch_two, True), (hidden_one, True), (down_bias_row, False), (own_mod, True),
            (own_keep, True), (grad_two, True), (picks_row, True), (image_tokens, True),
        ],
        [((images, patches, width), BF16), ((images, 1, width), F32)],
    )
    qkv_grad, mixed_grad, attend_stats, bias_sums = call(
        functools.partial(attend_back_body, head_dim), group,
        [
            (group_grad, True), (qkv, True), (group_routed, True), (keep, True),
            (qkv_weight, False), (out_weight, False),
        ],
        [
            ((group, 3, slots, cols), BF16), (group_shape, BF16), ((group, 3, width), F32),
            ((group, 2, cols), F32),
        ],
    )
    mixed_one_grad = own_sum(mixed_grad)
    sums = [join(after(own, attend_stats), got, way[1]) for (own, got), way in zip(flights, ways)]
    up_weight_grad, down_weight_grad = [
        join(*double(part, way[0]), way[0]) for part, way in zip(sums, ways)
    ]

    qkv_part = jnp.einsum(
        "gtsc,gsd->tcd", qkv_grad, mixed_one, preferred_element_type=F32
    ).reshape(3 * cols, width)
    out_part = mm(attended.reshape(-1, cols), group_grad.reshape(wide), TN)
    part = jnp.concatenate([qkv_part.astype(BF16), out_part.astype(BF16)], axis=0)
    part = jnp.concatenate(sum_pair((part[: 2 * cols], part[2 * cols :])), axis=0)
    qkv_weight_grad = part[: 3 * cols].reshape(3, cols, width)
    out_weight_grad = part[3 * cols :]

    own_rows = jnp.concatenate([middle_stats, gate_grad], axis=1)
    placed = lax.dynamic_update_slice(
        jnp.zeros((group, 4, width), F32), own_rows, (here * images, 0, 0)
    )
    mod_grad = jnp.concatenate([attend_stats[:, :2], placed], axis=1)
    each = 6 * width // (groups * members)
    mod_grad = mod_grad.reshape(group, groups, members, each)
    mod_grad = small_scatter_sum(mod_grad.transpose(2, 0, 1, 3)).astype(BF16)
    pieces = [
        mod_grad.reshape(-1),
        silu_cond.reshape(-1),
        jnp.sum(bias_sums, axis=0).astype(BF16).reshape(-1),
        jnp.sum(attend_stats[:, 2], axis=0).astype(BF16),
        jnp.sum(up_sum, axis=0).astype(BF16).reshape(-1),
        jnp.sum(down_sum, axis=0).astype(BF16).reshape(-1),
    ]
    sizes = [piece.shape[0] for piece in pieces]
    packed = jnp.concatenate(pieces)
    packed = jnp.pad(packed, (0, -packed.shape[0] % 2048)).reshape(-1, 128)
    packed = lax.all_gather(packed, "dp", axis=0, tiled=False).reshape(groups, -1)
    starts = [sum(sizes[:i]) for i in range(len(sizes))]
    views = [packed[:, s : s + n] for s, n in zip(starts, sizes)]
    mod_all = views[0].reshape(groups, group, groups, each)
    mod_all = lax.dynamic_index_in_dim(mod_all, lax.axis_index("dp"), 2, keepdims=False)
    mod_all = mod_all.reshape(groups * group, each)
    cond_all = views[1].reshape(groups * group, width)
    ada_weight_grad = mm(mod_all, cond_all, TN)
    ada_bias_grad = jnp.sum(mod_all.astype(F32), axis=0)
    qv_sum, out_sum, up_bias_grad, down_bias_grad = [
        jnp.sum(view.astype(F32), axis=0) for view in views[2:]
    ]

    tokens_grad = call(
        first_back_body, images,
        [
            (mixed_one_grad, True), (routed, True), (own_mod, True), (grad_one, True),
            (after(picks_row, ada_weight_grad), True), (image_cot, True),
        ],
        [((images, patches, width), BF16)],
    )[0]
    return (
        layer_out.reshape(images * patches, width),
        tokens_grad.reshape(images * patches, width),
        ada_weight_grad,
        ada_bias_grad,
        qkv_weight_grad.astype(F32),
        qv_sum.reshape(2, cols),
        out_weight_grad.astype(F32),
        out_sum,
        up_weight_grad.astype(F32),
        up_bias_grad,
        down_weight_grad.astype(F32),
        down_bias_grad,
    )


def solution(mesh):
    both = ("dp", "mp")
    in_specs = (
        P(both, None), P(both, None), P(both, None), P(both), P(both, None), P(), P(),
        P(None, "mp", None), P(None, "mp"), P("mp", None), P(), P("mp", None), P("mp"),
        P("mp", None), P(),
    )
    out_specs = (
        P(both, None), P(both, None), P(both, None), P(both), P(None, "mp", None), P(None, "mp"),
        P("mp", None), P(), P("mp", None), P("mp"), P("mp", None), P(),
    )

    return jax.shard_map(
        per_device, mesh=mesh, in_specs=in_specs, out_specs=out_specs, check_vma=False
    )
```

```python
import functools
import math

import jax
import jax.numpy as jnp
from jax import lax
from jax.experimental import pallas as pl
from jax.experimental.pallas import tpu as pltpu
from jax.sharding import PartitionSpec as P


HEADS = 16
EPS = 1e-06
F32 = jnp.float32
BF16 = jnp.bfloat16
GELU_A = math.sqrt(2.0 / math.pi)
GELU_B = 0.044715


def norm_rows(rows):
    mean = jnp.mean(rows, axis=-1, keepdims=True)
    centred = rows - mean
    rstd = lax.rsqrt(jnp.mean(centred * centred, axis=-1, keepdims=True) + EPS)
    return centred * rstd, rstd


def norm_back(normed, rstd, grad):
    return rstd * (
        grad
        - jnp.mean(grad, axis=-1, keepdims=True)
        - normed * jnp.mean(grad * normed, axis=-1, keepdims=True)
    )


def mm(left, right, dims=((1,), (0,))):
    return lax.dot_general(left, right, (dims, ((), ())), preferred_element_type=F32)


NT = ((1,), (1,))
TN = ((0,), (0,))


def block(shape):
    rank = len(shape)
    return pl.BlockSpec((1,) + tuple(shape[1:]), lambda i: (i,) + (0,) * (rank - 1))


def whole(shape):
    rank = len(shape)
    return pl.BlockSpec(tuple(shape), lambda i: (0,) * rank)


def call(body, grid, ins, outs, fixed=0, scratch=()):
    moving = len(outs) - fixed
    return pl.pallas_call(
        body,
        grid=(grid,),
        in_specs=[block(a.shape) if step else whole(a.shape) for a, step in ins],
        out_specs=[block(shape) for shape, _ in outs[:moving]]
        + [whole(shape) for shape, _ in outs[moving:]],
        scratch_shapes=list(scratch),
        out_shape=[jax.ShapeDtypeStruct(shape, dtype) for shape, dtype in outs],
    )(*[a for a, _ in ins])


def gather_body(picks, tokens, cotangent, routed, grad_two):
    slots, patches = routed.shape[1], tokens.shape[1]
    hot = (lax.broadcasted_iota(jnp.int32, (slots, patches), 1) == picks[0]).astype(F32)
    hot = hot.astype(BF16)
    routed[0] = mm(hot, tokens[0]).astype(BF16)
    grad_two[0] = mm(hot, cotangent[0]).astype(BF16)


def mod_row(mod, index):
    return mod[0][index : index + 1, :]


def live_rows(keep, slots):
    return (lax.broadcasted_iota(jnp.int32, (slots, 1), 0).astype(F32) < keep[0][:, :1]).astype(F32)


def live_keys(keep, slots):
    return lax.broadcasted_iota(jnp.int32, (1, slots), 1).astype(F32) < keep[0][:, :1]


def head_mask(head, head_dim, cols):
    lane = lax.broadcasted_iota(jnp.int32, (1, cols), 1)
    inside = jnp.logical_and(lane >= head * head_dim, lane < (head + 1) * head_dim)
    return inside.astype(F32).astype(BF16)


def softmax_of(query, key, alive, scale):
    scores = mm(query, key, NT) * scale
    scores = jnp.where(alive, scores, -1e30)
    raised = jnp.exp(scores - jnp.max(scores, axis=-1, keepdims=True))
    return raised / jnp.sum(raised, axis=-1, keepdims=True)


def attend_body(head_dim, routed, mod, keep, weight, bias, out_weight, mixed, qkv, attended, branch):
    slots, cols = routed.shape[1], weight.shape[1]
    scale = 1.0 / math.sqrt(head_dim)
    normed, _ = norm_rows(routed[0].astype(F32))
    rows = (normed * (1.0 + mod_row(mod, 1)) + mod_row(mod, 0)).astype(BF16)
    mixed[0] = rows
    query = (mm(rows, weight[0], NT) + bias[0:1, :]).astype(BF16)
    key = mm(rows, weight[1], NT).astype(BF16)
    value = (mm(rows, weight[2], NT) + bias[1:2, :]).astype(BF16)
    qkv[0, 0] = query
    qkv[0, 1] = key
    qkv[0, 2] = value
    alive = live_keys(keep, slots)
    total = jnp.zeros((slots, cols), F32)
    for head in range(cols // head_dim):
        mask = head_mask(head, head_dim, cols)
        low = softmax_of(query * mask, key, alive, scale).astype(BF16)
        total = total + mm(low, value * mask)
    total = total.astype(BF16)
    attended[0] = total
    branch[0] = mm(total, out_weight[...]).astype(BF16)


def attend_back_body(
    head_dim, grad, qkv, routed, mixed, attended, keep, weight, out_weight,
    mixed_grad, stats, bias_sums, part, total,
):
    slots, cols = routed.shape[1], weight.shape[1]
    scale = 1.0 / math.sqrt(head_dim)
    rows_grad = grad[0]
    attended_grad = mm(rows_grad, out_weight[...], NT).astype(BF16)
    query, key, value = qkv[0, 0], qkv[0, 1], qkv[0, 2]
    alive = live_keys(keep, slots)
    query_grad = jnp.zeros((slots, cols), F32)
    key_grad = jnp.zeros((slots, cols), F32)
    value_grad = jnp.zeros((slots, cols), F32)
    for head in range(cols // head_dim):
        mask = head_mask(head, head_dim, cols)
        own_query = query * mask
        weights = softmax_of(own_query, key, alive, scale)
        own_grad = attended_grad * mask
        weight_grad = mm(own_grad, value, NT)
        value_grad = value_grad + mm(weights.astype(BF16), own_grad, TN)
        row_total = jnp.sum(weights * weight_grad, axis=-1, keepdims=True)
        score_grad = (weights * (weight_grad - row_total)).astype(BF16)
        query_grad = query_grad + mm(score_grad, key * mask)
        key_grad = key_grad + mm(score_grad, own_query, TN)
    query_grad = (query_grad * scale).astype(BF16)
    key_grad = (key_grad * scale).astype(BF16)
    value_grad = value_grad.astype(BF16)
    step = pl.program_id(0)

    @pl.when(step == 0)
    def _():
        total[...] = jnp.zeros_like(total)

    total[0] += mm(query_grad, mixed[0], TN)
    total[1] += mm(key_grad, mixed[0], TN)
    total[2] += mm(value_grad, mixed[0], TN)
    total[3] += mm(attended[0], rows_grad, TN)

    @pl.when(step == pl.num_programs(0) - 1)
    def _():
        part[...] = total[...].astype(BF16)

    rows = mm(query_grad, weight[0]) + mm(key_grad, weight[1]) + mm(value_grad, weight[2])
    mixed_grad[0] = rows.astype(BF16)
    normed, _ = norm_rows(routed[0].astype(F32))
    stats[0, 0:1, :] = jnp.sum(rows, axis=0, keepdims=True)
    stats[0, 1:2, :] = jnp.sum(rows * normed, axis=0, keepdims=True)
    stats[0, 2:3, :] = jnp.sum(rows_grad.astype(F32), axis=0, keepdims=True)
    bias_sums[0, 0:1, :] = jnp.sum(query_grad.astype(F32), axis=0, keepdims=True)
    bias_sums[0, 1:2, :] = jnp.sum(value_grad.astype(F32), axis=0, keepdims=True)


def down_back_body(grad_two, mod, keep, down, down_grad, active_grad, down_sum):
    gate = live_rows(keep, grad_two.shape[1]) * mod_row(mod, 5)
    rows = (gate * grad_two[0].astype(F32)).astype(BF16)
    down_grad[0] = rows
    down_sum[0] = jnp.sum(rows.astype(F32), axis=0, keepdims=True)
    active_grad[0] = mm(rows, down[...], NT)


def forward_body(mixed, active_grad, up, up_bias, active, before_grad, mixed_grad, up_sum):
    units = up.shape[0]
    step = 384 if units % 384 == 0 else units
    rows = mixed[0]
    total = None
    for start in range(0, units, step):
        at = slice(start, start + step)
        before = mm(rows, up[at, :], NT) + up_bias[:, at]
        square = before * before
        tanh = jnp.tanh(GELU_A * (before + GELU_B * (before * square)))
        half = 0.5 * (1.0 + tanh)
        active[0, :, at] = (before * half).astype(BF16)
        slope = half + 0.5 * before * (1.0 - tanh * tanh) * (
            GELU_A * (1.0 + 3.0 * GELU_B * square)
        )
        inner = (active_grad[0, :, at] * slope).astype(BF16)
        before_grad[0, :, at] = inner
        up_sum[0, :, at] = jnp.sum(inner.astype(F32), axis=0, keepdims=True)
        piece = mm(inner, up[at, :])
        total = piece if total is None else total + piece
    mixed_grad[0] = total.astype(BF16)


def branch_body(active, grad_two, keep, down, bias, branch, gate_grad):
    rows = mm(active[0], down[...])
    branch[0] = rows.astype(BF16)
    grad = live_rows(keep, grad_two.shape[1]) * grad_two[0].astype(F32)
    gate_grad[0] = jnp.sum(grad * (rows + bias[...]), axis=0, keepdims=True)


def middle_body(branch, out_bias, routed, mod, keep, hidden, mixed):
    slots = routed.shape[1]
    branch_one = branch[0].astype(F32) + out_bias[...]
    rows = routed[0].astype(F32) + live_rows(keep, slots) * mod_row(mod, 2) * branch_one
    hidden[0] = rows
    normed, _ = norm_rows(rows)
    mixed[0] = (normed * (1.0 + mod_row(mod, 4)) + mod_row(mod, 3)).astype(BF16)


def middle_back_body(
    mixed_grad, hidden, branch, out_bias, grad_two, mod, keep, grad_one, branch_grad, stats
):
    slots = hidden.shape[1]
    rows = mixed_grad[0].astype(F32)
    normed, rstd = norm_rows(hidden[0])
    grad = grad_two[0].astype(F32) + norm_back(normed, rstd, rows * (1.0 + mod_row(mod, 4)))
    grad_one[0] = grad
    live = live_rows(keep, slots)
    branch_one = branch[0].astype(F32) + out_bias[...]
    stats[0, 0:1, :] = jnp.sum(live * grad * branch_one, axis=0, keepdims=True)
    stats[0, 1:2, :] = jnp.sum(rows, axis=0, keepdims=True)
    stats[0, 2:3, :] = jnp.sum(rows * normed, axis=0, keepdims=True)
    branch_grad[0] = (live * mod_row(mod, 2) * grad).astype(BF16)


def place(picks, base, rows):
    patches, slots = base.shape[0], rows.shape[0]
    hot = (lax.broadcasted_iota(jnp.int32, (patches, slots), 0) == picks).astype(F32)
    taken = jnp.max(hot, axis=1, keepdims=True) > 0
    return jnp.where(taken, mm(hot.astype(BF16), rows.astype(BF16)), base.astype(F32)).astype(BF16)


def out_body(branch, hidden, down_bias, mod, keep, picks, tokens, layer_out):
    branch_two = branch[0].astype(F32) + down_bias[...]
    rows = hidden[0] + live_rows(keep, hidden.shape[1]) * mod_row(mod, 5) * branch_two
    layer_out[0] = place(picks[0], tokens[0], rows)


def first_back_body(mixed_grad, routed, mod, grad_one, picks, cotangent, tokens_grad):
    normed, rstd = norm_rows(routed[0].astype(F32))
    rows = mixed_grad[0].astype(F32) * (1.0 + mod_row(mod, 1))
    tokens_grad[0] = place(picks[0], cotangent[0], grad_one[0] + norm_back(normed, rstd, rows))


def dp_bits():
    count = lax.axis_size("dp").bit_length() - 1
    return list(range(count))


def partner(bit):
    return [(i, i ^ (1 << bit)) for i in range(lax.axis_size("dp"))]


def halve(part, bit):
    side = (lax.axis_index("dp") >> bit) & 1
    halves = part.reshape(2, part.shape[0] // 2, part.shape[1])
    own = lax.dynamic_index_in_dim(halves, side, 0, keepdims=False)
    other = lax.dynamic_index_in_dim(halves, 1 - side, 0, keepdims=False)
    return own, lax.ppermute(other, "dp", partner(bit))


def add_low(own, got):
    return (own.astype(F32) + got.astype(F32)).astype(BF16)


def double(part, bit):
    return part, lax.ppermute(part, "dp", partner(bit))


def join(own, got, bit):
    side = (lax.axis_index("dp") >> bit) & 1
    return jnp.where(side == 0, jnp.concatenate([own, got], 0), jnp.concatenate([got, own], 0))


def after(value, *others):
    return lax.optimization_barrier((value,) + others)[0]


def halve_all(parts, level):
    ways = orders()
    flights = [halve(part, way[level]) for part, way in zip(parts, ways)]
    return [add_low(own, got) for own, got in lax.optimization_barrier(flights)]


def join_all(parts, level):
    ways = orders()
    flights = [double(part, way[level]) for part, way in zip(parts, ways)]
    flights = lax.optimization_barrier(flights)
    return [join(own, got, way[level]) for (own, got), way in zip(flights, ways)]


def orders():
    bits = dp_bits()
    return bits, bits[:1] + bits[2:] + bits[1:2]


def shift(value, step):
    count = lax.axis_size("mp")
    return lax.ppermute(value, "mp", [(i, (i + step) % count) for i in range(count)])


def small_gather(value):
    count, here = lax.axis_size("mp"), lax.axis_index("mp")
    rows = jnp.stack([value] + [shift(value, step) for step in range(1, count)])
    return jnp.take(rows, (here - jnp.arange(count)) % count, axis=0)


def small_scatter_sum(parts):
    count, here = lax.axis_size("mp"), lax.axis_index("mp")
    total = lax.dynamic_index_in_dim(parts, here, 0, keepdims=False)
    for step in range(1, count):
        to = (here + step) % count
        total = total + shift(lax.dynamic_index_in_dim(parts, to, 0, keepdims=False), step)
    return total


def all_rows(rows):
    return lax.all_gather(rows, "mp", axis=0, tiled=True)


def own_sum(rows):
    return lax.psum_scatter(rows, "mp", scatter_dimension=0, tiled=True)


def per_device(
    tokens, conditioning, routes, keep_count, cotangent, ada_weight, ada_bias, qkv_weight,
    qv_bias, out_weight, out_bias, up_weight, up_bias, down_weight, down_bias,
):
    images = conditioning.shape[0]
    width = tokens.shape[1]
    patches = routes.shape[1]
    slots = 3 * patches // 4
    cols = qkv_weight.shape[1]
    head_dim = width // HEADS
    hidden_units = up_weight.shape[0]
    members = lax.axis_size("mp")
    groups = lax.axis_size("dp")
    group = members * images
    here = lax.axis_index("mp")

    image_tokens = tokens.reshape(images, patches, width)
    image_cot = cotangent.reshape(images, patches, width)
    picks = routes[:, :slots]
    picks_col = picks.reshape(images, slots, 1)
    picks_row = picks.reshape(images, 1, slots)
    rows_shape = (images, slots, width)
    group_shape = (group, slots, width)

    routed, grad_two = call(
        gather_body, images,
        [(picks_col, True), (image_tokens, True), (image_cot, True)],
        [(rows_shape, BF16), (rows_shape, BF16)],
    )
    group_routed = all_rows(routed)
    group_two = all_rows(grad_two)

    small = jnp.concatenate(
        [conditioning, jnp.broadcast_to(keep_count.astype(BF16)[:, None], (images, 128))], axis=1
    )
    small = small_gather(small).reshape(group, width + 128)
    silu_cond = jax.nn.silu(small[:, :width].astype(F32)).astype(BF16)
    modulation = mm(silu_cond, ada_weight, NT) + ada_bias.astype(F32)
    modulation = modulation.reshape(group, 6, width)
    keep = small[:, None, width:].astype(F32)
    own_mod = lax.dynamic_slice_in_dim(modulation, here * images, images, 0)
    own_keep = jnp.broadcast_to(keep_count.astype(F32)[:, None, None], (images, 1, 128))
    out_bias_row = out_bias.astype(F32)[None]
    down_bias_row = down_bias.astype(F32)[None]

    mixed_one, qkv, attended, branch = call(
        functools.partial(attend_body, head_dim), group,
        [
            (group_routed, True), (modulation, True), (keep, True), (qkv_weight, False),
            (qv_bias.astype(F32), False), (out_weight, False),
        ],
        [
            (group_shape, BF16), ((group, 3, slots, cols), BF16), ((group, slots, cols), BF16),
            (group_shape, BF16),
        ],
    )
    branch_one = own_sum(branch)
    hidden_one, mixed_two = call(
        middle_body, images,
        [
            (branch_one, True), (out_bias_row, False), (routed, True), (own_mod, True),
            (own_keep, True),
        ],
        [(rows_shape, F32), (rows_shape, BF16)],
    )
    group_mixed = all_rows(mixed_two)
    unit_shape = (group, slots, hidden_units)
    down_grad, active_grad, down_sum = call(
        down_back_body, group,
        [(group_two, True), (modulation, True), (keep, True), (down_weight, False)],
        [(group_shape, BF16), (unit_shape, F32), ((group, 1, width), F32)],
    )
    active, before_grad, mixed_grad, up_sum = call(
        forward_body, group,
        [
            (group_mixed, True), (active_grad, True), (up_weight, False),
            (up_bias.astype(F32)[None], False),
        ],
        [
            (unit_shape, BF16), (unit_shape, BF16), (group_shape, BF16),
            ((group, 1, hidden_units), F32),
        ],
    )
    mixed_two_grad = own_sum(mixed_grad)
    flat = (group * slots, hidden_units)
    wide = (group * slots, width)
    up_part = mm(before_grad.reshape(flat), group_mixed.reshape(wide), TN).astype(BF16)
    down_part = mm(active.reshape(flat), down_grad.reshape(wide), TN).astype(BF16)
    levels = len(dp_bits())
    sums = halve_all((up_part, down_part), 0)
    branch, gate_grad = call(
        branch_body, group,
        [
            (active, True), (group_two, True), (after(keep, *sums), True), (down_weight, False),
            (jnp.where(here == 0, down_bias_row, 0.0), False),
        ],
        [(group_shape, BF16), ((group, 1, width), F32)],
    )
    sums = halve_all(sums, 1)

    grad_one, branch_grad, middle_stats = call(
        middle_back_body, images,
        [
            (mixed_two_grad, True), (hidden_one, True), (branch_one, True), (out_bias_row, False),
            (grad_two, True), (own_mod, True), (after(own_keep, gate_grad, *sums), True),
        ],
        [(rows_shape, F32), (rows_shape, BF16), ((images, 3, width), F32)],
    )
    group_grad = all_rows(branch_grad)
    branch_two = own_sum(branch)
    for level in range(2, levels):
        sums = halve_all(sums, level)
    for level in reversed(range(1, levels)):
        sums = join_all(sums, level)
    up_weight_grad, down_weight_grad = [part.astype(F32) for part in join_all(sums, 0)]
    mixed_grad, attend_stats, bias_sums, part = call(
        functools.partial(attend_back_body, head_dim), group,
        [
            (group_grad, True), (qkv, True), (group_routed, True), (mixed_one, True),
            (attended, True), (after(keep, up_weight_grad, down_weight_grad), True),
            (qkv_weight, False), (out_weight, False),
        ],
        [
            (group_shape, BF16), ((group, 3, width), F32), ((group, 2, cols), F32),
            ((4, cols, width), BF16),
        ],
        fixed=1,
        scratch=[pltpu.VMEM((4, cols, width), F32)],
    )
    (layer_out,) = call(
        out_body, images,
        [
            (branch_two, True), (hidden_one, True), (down_bias_row, False), (own_mod, True),
            (after(own_keep, attend_stats), True), (picks_row, True), (image_tokens, True),
        ],
        [((images, patches, width), BF16)],
    )
    mixed_one_grad = own_sum(mixed_grad)
    part = part.reshape(2, 2 * cols, width)
    firsts = [part[0], part[1]]
    for level in range(levels):
        firsts = halve_all(firsts, level)
    for level in reversed(range(levels)):
        firsts = join_all(firsts, level)
    part = jnp.concatenate(firsts, axis=0).astype(F32)
    qkv_weight_grad = part[: 3 * cols].reshape(3, cols, width)
    out_weight_grad = part[3 * cols :]

    placed = lax.dynamic_update_slice(
        jnp.zeros((group, 3, width), F32), middle_stats, (here * images, 0, 0)
    )
    mod_grad = jnp.concatenate([attend_stats[:, :2], placed, gate_grad], axis=1)
    each = 6 * width // (groups * members)
    mod_grad = mod_grad.reshape(group, groups, members, each)
    mod_grad = small_scatter_sum(mod_grad.transpose(2, 0, 1, 3)).astype(BF16)
    pieces = [
        mod_grad.reshape(-1),
        silu_cond.reshape(-1),
        jnp.sum(bias_sums, axis=0).astype(BF16).reshape(-1),
        jnp.sum(attend_stats[:, 2], axis=0).astype(BF16),
        jnp.sum(up_sum, axis=0).astype(BF16).reshape(-1),
        jnp.sum(down_sum, axis=0).astype(BF16).reshape(-1),
    ]
    sizes = [piece.shape[0] for piece in pieces]
    packed = jnp.concatenate(pieces)
    packed = jnp.pad(packed, (0, -packed.shape[0] % 2048)).reshape(-1, 128)
    packed = lax.all_gather(packed, "dp", axis=0, tiled=False).reshape(groups, -1)
    starts = [sum(sizes[:i]) for i in range(len(sizes))]
    views = [packed[:, s : s + n] for s, n in zip(starts, sizes)]
    mod_all = views[0].reshape(groups, group, groups, each)
    mod_all = lax.dynamic_index_in_dim(mod_all, lax.axis_index("dp"), 2, keepdims=False)
    mod_all = mod_all.reshape(groups * group, each)
    cond_all = views[1].reshape(groups * group, width)
    ada_weight_grad = mm(mod_all, cond_all, TN)
    ada_bias_grad = jnp.sum(mod_all.astype(F32), axis=0)
    qv_sum, out_sum, up_bias_grad, down_bias_grad = [
        jnp.sum(view.astype(F32), axis=0) for view in views[2:]
    ]

    tokens_grad = call(
        first_back_body, images,
        [
            (mixed_one_grad, True), (routed, True), (own_mod, True), (grad_one, True),
            (after(picks_row, ada_weight_grad), True), (image_cot, True),
        ],
        [((images, patches, width), BF16)],
    )[0]
    return (
        layer_out.reshape(images * patches, width),
        tokens_grad.reshape(images * patches, width),
        ada_weight_grad,
        ada_bias_grad,
        qkv_weight_grad,
        qv_sum.reshape(2, cols),
        out_weight_grad,
        out_sum,
        up_weight_grad,
        up_bias_grad,
        down_weight_grad,
        down_bias_grad,
    )


def solution(mesh):
    both = ("dp", "mp")
    in_specs = (
        P(both, None), P(both, None), P(both, None), P(both), P(both, None), P(), P(),
        P(None, "mp", None), P(None, "mp"), P("mp", None), P(), P("mp", None), P("mp"),
        P("mp", None), P(),
    )
    out_specs = (
        P(both, None), P(both, None), P(both, None), P(both), P(None, "mp", None), P(None, "mp"),
        P("mp", None), P(), P("mp", None), P("mp"), P("mp", None), P(),
    )

    return jax.shard_map(
        per_device, mesh=mesh, in_specs=in_specs, out_specs=out_specs, check_vma=False
    )
```

```python
import functools
import math

import jax
import jax.numpy as jnp
from jax import lax
from jax.experimental import pallas as pl
from jax.experimental.pallas import tpu as pltpu
from jax.sharding import PartitionSpec as P


HEADS = 16
EPS = 1e-06
F32 = jnp.float32
BF16 = jnp.bfloat16
GELU_A = math.sqrt(2.0 / math.pi)
GELU_B = 0.044715


def norm_rows(rows):
    mean = jnp.mean(rows, axis=-1, keepdims=True)
    centred = rows - mean
    rstd = lax.rsqrt(jnp.mean(centred * centred, axis=-1, keepdims=True) + EPS)
    return centred * rstd, rstd


def norm_back(normed, rstd, grad):
    return rstd * (
        grad
        - jnp.mean(grad, axis=-1, keepdims=True)
        - normed * jnp.mean(grad * normed, axis=-1, keepdims=True)
    )


def mm(left, right, dims=((1,), (0,))):
    return lax.dot_general(left, right, (dims, ((), ())), preferred_element_type=F32)


NT = ((1,), (1,))
TN = ((0,), (0,))


def block(shape):
    rank = len(shape)
    return pl.BlockSpec((1,) + tuple(shape[1:]), lambda i: (i,) + (0,) * (rank - 1))


def whole(shape):
    rank = len(shape)
    return pl.BlockSpec(tuple(shape), lambda i: (0,) * rank)


def call(body, grid, ins, outs, fixed=0, scratch=()):
    moving = len(outs) - fixed
    return pl.pallas_call(
        body,
        grid=(grid,),
        in_specs=[block(a.shape) if step else whole(a.shape) for a, step in ins],
        out_specs=[block(shape) for shape, _ in outs[:moving]]
        + [whole(shape) for shape, _ in outs[moving:]],
        scratch_shapes=list(scratch),
        out_shape=[jax.ShapeDtypeStruct(shape, dtype) for shape, dtype in outs],
    )(*[a for a, _ in ins])


def gather_body(picks, tokens, cotangent, routed, grad_two):
    slots, patches = routed.shape[1], tokens.shape[1]
    hot = (lax.broadcasted_iota(jnp.int32, (slots, patches), 1) == picks[0]).astype(F32)
    hot = hot.astype(BF16)
    routed[0] = mm(hot, tokens[0]).astype(BF16)
    grad_two[0] = mm(hot, cotangent[0]).astype(BF16)


def mod_row(mod, index):
    return mod[0][index : index + 1, :]


def live_rows(keep, slots):
    return (lax.broadcasted_iota(jnp.int32, (slots, 1), 0).astype(F32) < keep[0][:, :1]).astype(F32)


def live_keys(keep, slots):
    return lax.broadcasted_iota(jnp.int32, (1, slots), 1).astype(F32) < keep[0][:, :1]


def head_mask(head, head_dim, cols):
    lane = lax.broadcasted_iota(jnp.int32, (1, cols), 1)
    inside = jnp.logical_and(lane >= head * head_dim, lane < (head + 1) * head_dim)
    return inside.astype(F32).astype(BF16)


def softmax_of(query, key, alive, scale):
    scores = mm(query, key, NT) * scale
    scores = jnp.where(alive, scores, -1e30)
    raised = jnp.exp(scores - jnp.max(scores, axis=-1, keepdims=True))
    return raised / jnp.sum(raised, axis=-1, keepdims=True)


def attend_body(head_dim, routed, mod, keep, weight, bias, out_weight, mixed, qkv, attended, branch):
    slots, cols = routed.shape[1], weight.shape[1]
    scale = 1.0 / math.sqrt(head_dim)
    normed, _ = norm_rows(routed[0].astype(F32))
    rows = (normed * (1.0 + mod_row(mod, 1)) + mod_row(mod, 0)).astype(BF16)
    mixed[0] = rows
    query = (mm(rows, weight[0], NT) + bias[0:1, :]).astype(BF16)
    key = mm(rows, weight[1], NT).astype(BF16)
    value = (mm(rows, weight[2], NT) + bias[1:2, :]).astype(BF16)
    qkv[0, 0] = query
    qkv[0, 1] = key
    qkv[0, 2] = value
    alive = live_keys(keep, slots)
    total = jnp.zeros((slots, cols), F32)
    for head in range(cols // head_dim):
        mask = head_mask(head, head_dim, cols)
        low = softmax_of(query * mask, key, alive, scale).astype(BF16)
        total = total + mm(low, value * mask)
    total = total.astype(BF16)
    attended[0] = total
    branch[0] = mm(total, out_weight[...]).astype(BF16)


def attend_back_body(
    head_dim, grad, qkv, routed, mixed, attended, keep, weight, out_weight,
    mixed_grad, stats, bias_sums, part, total,
):
    slots, cols = routed.shape[1], weight.shape[1]
    scale = 1.0 / math.sqrt(head_dim)
    rows_grad = grad[0]
    attended_grad = mm(rows_grad, out_weight[...], NT).astype(BF16)
    query, key, value = qkv[0, 0], qkv[0, 1], qkv[0, 2]
    alive = live_keys(keep, slots)
    query_grad = jnp.zeros((slots, cols), F32)
    key_grad = jnp.zeros((slots, cols), F32)
    value_grad = jnp.zeros((slots, cols), F32)
    for head in range(cols // head_dim):
        mask = head_mask(head, head_dim, cols)
        own_query = query * mask
        weights = softmax_of(own_query, key, alive, scale)
        own_grad = attended_grad * mask
        weight_grad = mm(own_grad, value, NT)
        value_grad = value_grad + mm(weights.astype(BF16), own_grad, TN)
        row_total = jnp.sum(weights * weight_grad, axis=-1, keepdims=True)
        score_grad = (weights * (weight_grad - row_total)).astype(BF16)
        query_grad = query_grad + mm(score_grad, key * mask)
        key_grad = key_grad + mm(score_grad, own_query, TN)
    query_grad = (query_grad * scale).astype(BF16)
    key_grad = (key_grad * scale).astype(BF16)
    value_grad = value_grad.astype(BF16)
    step = pl.program_id(0)

    @pl.when(step == 0)
    def _():
        total[...] = jnp.zeros_like(total)

    total[0] += mm(query_grad, mixed[0], TN)
    total[1] += mm(key_grad, mixed[0], TN)
    total[2] += mm(value_grad, mixed[0], TN)
    total[3] += mm(attended[0], rows_grad, TN)

    @pl.when(step == pl.num_programs(0) - 1)
    def _():
        part[...] = total[...].astype(BF16)

    rows = mm(query_grad, weight[0]) + mm(key_grad, weight[1]) + mm(value_grad, weight[2])
    mixed_grad[0] = rows.astype(BF16)
    normed, _ = norm_rows(routed[0].astype(F32))
    stats[0, 0:1, :] = jnp.sum(rows, axis=0, keepdims=True)
    stats[0, 1:2, :] = jnp.sum(rows * normed, axis=0, keepdims=True)
    stats[0, 2:3, :] = jnp.sum(rows_grad.astype(F32), axis=0, keepdims=True)
    bias_sums[0, 0:1, :] = jnp.sum(query_grad.astype(F32), axis=0, keepdims=True)
    bias_sums[0, 1:2, :] = jnp.sum(value_grad.astype(F32), axis=0, keepdims=True)


def down_back_body(grad_two, mod, keep, down, down_grad, active_grad, down_sum):
    gate = live_rows(keep, grad_two.shape[1]) * mod_row(mod, 5)
    rows = (gate * grad_two[0].astype(F32)).astype(BF16)
    down_grad[0] = rows
    down_sum[0] = jnp.sum(rows.astype(F32), axis=0, keepdims=True)
    active_grad[0] = mm(rows, down[...], NT)


def forward_body(mixed, active_grad, up, up_bias, active, before_grad, mixed_grad, up_sum):
    units = up.shape[0]
    step = 384 if units % 384 == 0 else units
    rows = mixed[0]
    total = None
    for start in range(0, units, step):
        at = slice(start, start + step)
        before = mm(rows, up[at, :], NT) + up_bias[:, at]
        square = before * before
        tanh = jnp.tanh(GELU_A * (before + GELU_B * (before * square)))
        half = 0.5 * (1.0 + tanh)
        active[0, :, at] = (before * half).astype(BF16)
        slope = half + 0.5 * before * (1.0 - tanh * tanh) * (
            GELU_A * (1.0 + 3.0 * GELU_B * square)
        )
        inner = (active_grad[0, :, at] * slope).astype(BF16)
        before_grad[0, :, at] = inner
        up_sum[0, :, at] = jnp.sum(inner.astype(F32), axis=0, keepdims=True)
        piece = mm(inner, up[at, :])
        total = piece if total is None else total + piece
    mixed_grad[0] = total.astype(BF16)


def branch_body(active, grad_two, keep, down, bias, branch, gate_grad):
    rows = mm(active[0], down[...])
    branch[0] = rows.astype(BF16)
    grad = live_rows(keep, grad_two.shape[1]) * grad_two[0].astype(F32)
    gate_grad[0] = jnp.sum(grad * (rows + bias[...]), axis=0, keepdims=True)


def middle_body(branch, out_bias, routed, mod, keep, hidden, mixed):
    slots = routed.shape[1]
    branch_one = branch[0].astype(F32) + out_bias[...]
    rows = routed[0].astype(F32) + live_rows(keep, slots) * mod_row(mod, 2) * branch_one
    hidden[0] = rows
    normed, _ = norm_rows(rows)
    mixed[0] = (normed * (1.0 + mod_row(mod, 4)) + mod_row(mod, 3)).astype(BF16)


def middle_back_body(
    mixed_grad, hidden, branch, out_bias, grad_two, mod, keep, grad_one, branch_grad, stats
):
    slots = hidden.shape[1]
    rows = mixed_grad[0].astype(F32)
    normed, rstd = norm_rows(hidden[0])
    grad = grad_two[0].astype(F32) + norm_back(normed, rstd, rows * (1.0 + mod_row(mod, 4)))
    grad_one[0] = grad
    live = live_rows(keep, slots)
    branch_one = branch[0].astype(F32) + out_bias[...]
    stats[0, 0:1, :] = jnp.sum(live * grad * branch_one, axis=0, keepdims=True)
    stats[0, 1:2, :] = jnp.sum(rows, axis=0, keepdims=True)
    stats[0, 2:3, :] = jnp.sum(rows * normed, axis=0, keepdims=True)
    branch_grad[0] = (live * mod_row(mod, 2) * grad).astype(BF16)


def place(picks, base, rows):
    patches, slots = base.shape[0], rows.shape[0]
    hot = (lax.broadcasted_iota(jnp.int32, (patches, slots), 0) == picks).astype(F32)
    taken = jnp.max(hot, axis=1, keepdims=True) > 0
    return jnp.where(taken, mm(hot.astype(BF16), rows.astype(BF16)), base.astype(F32)).astype(BF16)


def out_body(branch, hidden, down_bias, mod, keep, picks, tokens, layer_out):
    branch_two = branch[0].astype(F32) + down_bias[...]
    rows = hidden[0] + live_rows(keep, hidden.shape[1]) * mod_row(mod, 5) * branch_two
    layer_out[0] = place(picks[0], tokens[0], rows)


def first_back_body(mixed_grad, routed, mod, grad_one, picks, cotangent, tokens_grad):
    normed, rstd = norm_rows(routed[0].astype(F32))
    rows = mixed_grad[0].astype(F32) * (1.0 + mod_row(mod, 1))
    tokens_grad[0] = place(picks[0], cotangent[0], grad_one[0] + norm_back(normed, rstd, rows))


def dp_bits():
    count = lax.axis_size("dp").bit_length() - 1
    return list(range(count))


def partner(bit):
    return [(i, i ^ (1 << bit)) for i in range(lax.axis_size("dp"))]


def halve(part, bit):
    side = (lax.axis_index("dp") >> bit) & 1
    halves = part.reshape(2, part.shape[0] // 2, part.shape[1])
    own = lax.dynamic_index_in_dim(halves, side, 0, keepdims=False)
    other = lax.dynamic_index_in_dim(halves, 1 - side, 0, keepdims=False)
    return own, lax.ppermute(other, "dp", partner(bit))


def add_low(own, got):
    return (own.astype(F32) + got.astype(F32)).astype(BF16)


def double(part, bit):
    return part, lax.ppermute(part, "dp", partner(bit))


def join(own, got, bit):
    side = (lax.axis_index("dp") >> bit) & 1
    return jnp.where(side == 0, jnp.concatenate([own, got], 0), jnp.concatenate([got, own], 0))


def after(value, *others):
    return lax.optimization_barrier((value,) + others)[0]


def halve_all(parts, level):
    ways = orders()
    flights = [halve(part, way[level]) for part, way in zip(parts, ways)]
    return [add_low(own, got) for own, got in lax.optimization_barrier(flights)]


def double_all(parts, level):
    flights = [double(part, way[level]) for part, way in zip(parts, orders())]
    return lax.optimization_barrier(flights)


def join_all(flights, level):
    return [join(own, got, way[level]) for (own, got), way in zip(flights, orders())]


def trade(part):
    count, mine = lax.axis_size("dp") // 2, lax.axis_index("dp") >> 1
    blocks = part.reshape(count, part.shape[0] // count, part.shape[1])
    own = lax.dynamic_index_in_dim(blocks, mine, 0, keepdims=False)
    sends = [
        lax.dynamic_index_in_dim(blocks, mine ^ step, 0, keepdims=False) for step in range(1, count)
    ]
    return [own] + far(sends)


def far(sends):
    every = range(lax.axis_size("dp"))
    return [
        lax.ppermute(send, "dp", [(i, i ^ (2 * step)) for i in every])
        for step, send in enumerate(sends, 1)
    ]


def spread(block):
    return [block] + far([block] * (lax.axis_size("dp") // 2 - 1))


def finish_body(places, own, got, first, second):
    count, rows = own.shape[0], first.shape[1]
    cut = first.shape[0]
    side, mine = places[0], places[1]

    def block(step):
        place = (step % count) ^ mine
        left, right = own[place, :rows, :], got[place, :rows, :]
        return jnp.where(step // count == side, left, right).astype(F32)

    def fill_first(step, carry):
        first[step] = block(step)
        return carry

    def fill_second(step, carry):
        second[step] = block(step + cut)
        return carry

    lax.fori_loop(0, cut, fill_first, 0)
    lax.fori_loop(0, 2 * count - cut, fill_second, 0)


def finish(own, got, rows):
    count, _, width = own.shape
    index = lax.axis_index("dp")
    places = jnp.stack([index & 1, index >> 1]).astype(jnp.int32)
    cut = 3 * count // 2
    vmem = pl.BlockSpec(memory_space=pltpu.VMEM)
    return pl.pallas_call(
        finish_body,
        in_specs=[pl.BlockSpec(memory_space=pltpu.SMEM), vmem, vmem],
        out_specs=[vmem, vmem],
        out_shape=[
            jax.ShapeDtypeStruct((cut, rows, width), F32),
            jax.ShapeDtypeStruct((2 * count - cut, rows, width), F32),
        ],
        name="finish",
    )(places, own, got)


def orders():
    bits = dp_bits()
    return bits, bits[:1] + bits[2:] + bits[1:2]


def shift(value, step):
    count = lax.axis_size("mp")
    return lax.ppermute(value, "mp", [(i, (i + step) % count) for i in range(count)])


def small_gather(value):
    count, here = lax.axis_size("mp"), lax.axis_index("mp")
    rows = jnp.stack([value] + [shift(value, step) for step in range(1, count)])
    return jnp.take(rows, (here - jnp.arange(count)) % count, axis=0)


def small_scatter_sum(parts):
    count, here = lax.axis_size("mp"), lax.axis_index("mp")
    total = lax.dynamic_index_in_dim(parts, here, 0, keepdims=False)
    for step in range(1, count):
        to = (here + step) % count
        total = total + shift(lax.dynamic_index_in_dim(parts, to, 0, keepdims=False), step)
    return total


def all_rows(rows):
    return lax.all_gather(rows, "mp", axis=0, tiled=True)


def own_sum(rows):
    return lax.psum_scatter(rows, "mp", scatter_dimension=0, tiled=True)


def per_device(
    tokens, conditioning, routes, keep_count, cotangent, ada_weight, ada_bias, qkv_weight,
    qv_bias, out_weight, out_bias, up_weight, up_bias, down_weight, down_bias,
):
    images = conditioning.shape[0]
    width = tokens.shape[1]
    patches = routes.shape[1]
    slots = 3 * patches // 4
    cols = qkv_weight.shape[1]
    head_dim = width // HEADS
    hidden_units = up_weight.shape[0]
    members = lax.axis_size("mp")
    groups = lax.axis_size("dp")
    group = members * images
    here = lax.axis_index("mp")

    image_tokens = tokens.reshape(images, patches, width)
    image_cot = cotangent.reshape(images, patches, width)
    picks = routes[:, :slots]
    picks_col = picks.reshape(images, slots, 1)
    picks_row = picks.reshape(images, 1, slots)
    rows_shape = (images, slots, width)
    group_shape = (group, slots, width)

    routed, grad_two = call(
        gather_body, images,
        [(picks_col, True), (image_tokens, True), (image_cot, True)],
        [(rows_shape, BF16), (rows_shape, BF16)],
    )
    group_routed = all_rows(routed)
    group_two = all_rows(grad_two)

    small = jnp.concatenate(
        [conditioning, jnp.broadcast_to(keep_count.astype(BF16)[:, None], (images, 128))], axis=1
    )
    small = small_gather(small).reshape(group, width + 128)
    silu_cond = jax.nn.silu(small[:, :width].astype(F32)).astype(BF16)
    modulation = mm(silu_cond, ada_weight, NT) + ada_bias.astype(F32)
    modulation = modulation.reshape(group, 6, width)
    keep = small[:, None, width:].astype(F32)
    own_mod = lax.dynamic_slice_in_dim(modulation, here * images, images, 0)
    own_keep = jnp.broadcast_to(keep_count.astype(F32)[:, None, None], (images, 1, 128))
    out_bias_row = out_bias.astype(F32)[None]
    down_bias_row = down_bias.astype(F32)[None]

    mixed_one, qkv, attended, branch = call(
        functools.partial(attend_body, head_dim), group,
        [
            (group_routed, True), (modulation, True), (keep, True), (qkv_weight, False),
            (qv_bias.astype(F32), False), (out_weight, False),
        ],
        [
            (group_shape, BF16), ((group, 3, slots, cols), BF16), ((group, slots, cols), BF16),
            (group_shape, BF16),
        ],
    )
    branch_one = own_sum(branch)
    hidden_one, mixed_two = call(
        middle_body, images,
        [
            (branch_one, True), (out_bias_row, False), (routed, True), (own_mod, True),
            (own_keep, True),
        ],
        [(rows_shape, F32), (rows_shape, BF16)],
    )
    group_mixed = all_rows(mixed_two)
    unit_shape = (group, slots, hidden_units)
    down_grad, active_grad, down_sum = call(
        down_back_body, group,
        [(group_two, True), (modulation, True), (keep, True), (down_weight, False)],
        [(group_shape, BF16), (unit_shape, F32), ((group, 1, width), F32)],
    )
    active, before_grad, mixed_grad, up_sum = call(
        forward_body, group,
        [
            (group_mixed, True), (active_grad, True), (up_weight, False),
            (up_bias.astype(F32)[None], False),
        ],
        [
            (unit_shape, BF16), (unit_shape, BF16), (group_shape, BF16),
            ((group, 1, hidden_units), F32),
        ],
    )
    mixed_two_grad = own_sum(mixed_grad)
    flat = (group * slots, hidden_units)
    wide = (group * slots, width)
    up_part = mm(before_grad.reshape(flat), group_mixed.reshape(wide), TN).astype(BF16)
    down_part = mm(active.reshape(flat), down_grad.reshape(wide), TN).astype(BF16)
    levels = len(dp_bits())
    sums = halve_all((up_part, down_part), 0)
    branch, gate_grad = call(
        branch_body, group,
        [
            (active, True), (group_two, True), (after(keep, *sums), True), (down_weight, False),
            (jnp.where(here == 0, down_bias_row, 0.0), False),
        ],
        [(group_shape, BF16), ((group, 1, width), F32)],
    )
    sums = halve_all(sums, 1)

    grad_one, branch_grad, middle_stats = call(
        middle_back_body, images,
        [
            (mixed_two_grad, True), (hidden_one, True), (branch_one, True), (out_bias_row, False),
            (grad_two, True), (own_mod, True), (after(own_keep, gate_grad, *sums), True),
        ],
        [(rows_shape, F32), (rows_shape, BF16), ((images, 3, width), F32)],
    )
    group_grad = all_rows(branch_grad)
    branch_two = own_sum(branch)
    for level in range(2, levels):
        sums = halve_all(sums, level)
    for level in reversed(range(1, levels)):
        sums = join_all(double_all(sums, level), level)
    last = double_all(sums, 0)
    mixed_grad, attend_stats, bias_sums, part = call(
        functools.partial(attend_back_body, head_dim), group,
        [
            (group_grad, True), (qkv, True), (group_routed, True), (mixed_one, True),
            (attended, True), (after(keep, last), True),
            (qkv_weight, False), (out_weight, False),
        ],
        [
            (group_shape, BF16), ((group, 3, width), F32), ((group, 2, cols), F32),
            ((4, cols, width), BF16),
        ],
        fixed=1,
        scratch=[pltpu.VMEM((4, cols, width), F32)],
    )
    (layer_out,) = call(
        out_body, images,
        [
            (branch_two, True), (hidden_one, True), (down_bias_row, False), (own_mod, True),
            (after(own_keep, attend_stats), True), (picks_row, True), (image_tokens, True),
        ],
        [((images, patches, width), BF16)],
    )
    mixed_one_grad = own_sum(mixed_grad)
    half = add_low(*halve(part.reshape(4 * cols, width), 0))
    last = after(last, half)
    blocks = trade(half)

    placed = lax.dynamic_update_slice(
        jnp.zeros((group, 3, width), F32), middle_stats, (here * images, 0, 0)
    )
    mod_grad = jnp.concatenate([attend_stats[:, :2], placed, gate_grad], axis=1)
    each = 6 * width // (groups * members)
    mod_grad = mod_grad.reshape(group, groups, members, each)
    mod_grad = small_scatter_sum(mod_grad.transpose(2, 0, 1, 3)).astype(BF16)
    pieces = [
        mod_grad.reshape(-1),
        silu_cond.reshape(-1),
        jnp.sum(bias_sums, axis=0).astype(BF16).reshape(-1),
        jnp.sum(attend_stats[:, 2], axis=0).astype(BF16),
        jnp.sum(up_sum, axis=0).astype(BF16).reshape(-1),
        jnp.sum(down_sum, axis=0).astype(BF16).reshape(-1),
    ]
    sizes = [piece.shape[0] for piece in pieces]
    packed = jnp.concatenate(pieces)
    packed = jnp.pad(packed, (0, -packed.shape[0] % (16 * width))).reshape(-1, width)
    blocks = after(blocks, packed)
    block_sum = sum(one.astype(F32) for one in blocks).astype(BF16)
    rows = block_sum.shape[0]
    last = after(last, block_sum)
    up_weight_grad, down_weight_grad = [one.astype(F32) for one in join_all(last, 0)]
    pieces = spread(jnp.concatenate([block_sum, packed]))
    own = jnp.stack(after(pieces, up_weight_grad, down_weight_grad, layer_out))
    own, got = double(own, 0)
    qkv_weight_grad, out_weight_grad = finish(own, got, rows)
    qkv_weight_grad = qkv_weight_grad.reshape(3, cols, width)
    out_weight_grad = out_weight_grad.reshape(cols, width)

    packed = jnp.stack([own[:, rows:], got[:, rows:]]).reshape(2, groups // 2, -1)
    place = lax.axis_index("dp")
    order = jnp.arange(groups) ^ place
    packed = packed[order & 1, order >> 1]
    starts = [sum(sizes[:i]) for i in range(len(sizes))]
    views = [packed[:, s : s + n] for s, n in zip(starts, sizes)]
    mod_all = views[0].reshape(groups, group, groups, each)
    mod_all = lax.dynamic_index_in_dim(mod_all, lax.axis_index("dp"), 2, keepdims=False)
    mod_all = mod_all.reshape(groups * group, each)
    cond_all = views[1].reshape(groups * group, width)
    ada_weight_grad = mm(mod_all, cond_all, TN)
    ada_bias_grad = jnp.sum(mod_all.astype(F32), axis=0)
    qv_sum, out_sum, up_bias_grad, down_bias_grad = [
        jnp.sum(view.astype(F32), axis=0) for view in views[2:]
    ]

    tokens_grad = call(
        first_back_body, images,
        [
            (mixed_one_grad, True), (routed, True), (own_mod, True), (grad_one, True),
            (after(picks_row, ada_weight_grad), True), (image_cot, True),
        ],
        [((images, patches, width), BF16)],
    )[0]
    return (
        layer_out.reshape(images * patches, width),
        tokens_grad.reshape(images * patches, width),
        ada_weight_grad,
        ada_bias_grad,
        qkv_weight_grad,
        qv_sum.reshape(2, cols),
        out_weight_grad,
        out_sum,
        up_weight_grad,
        up_bias_grad,
        down_weight_grad,
        down_bias_grad,
    )


def solution(mesh):
    both = ("dp", "mp")
    in_specs = (
        P(both, None), P(both, None), P(both, None), P(both), P(both, None), P(), P(),
        P(None, "mp", None), P(None, "mp"), P("mp", None), P(), P("mp", None), P("mp"),
        P("mp", None), P(),
    )
    out_specs = (
        P(both, None), P(both, None), P(both, None), P(both), P(None, "mp", None), P(None, "mp"),
        P("mp", None), P(), P("mp", None), P("mp"), P("mp", None), P(),
    )

    return jax.shard_map(
        per_device, mesh=mesh, in_specs=in_specs, out_specs=out_specs, check_vma=False
    )
```

```python
import functools
import math

import jax
import jax.numpy as jnp
from jax import lax
from jax.experimental import pallas as pl
from jax.experimental.pallas import tpu as pltpu
from jax.sharding import PartitionSpec as P


HEADS = 16
EPS = 1e-06
F32 = jnp.float32
BF16 = jnp.bfloat16
GELU_A = math.sqrt(2.0 / math.pi)
GELU_B = 0.044715


def norm_rows(rows):
    mean = jnp.mean(rows, axis=-1, keepdims=True)
    centred = rows - mean
    rstd = lax.rsqrt(jnp.mean(centred * centred, axis=-1, keepdims=True) + EPS)
    return centred * rstd, rstd


def norm_back(normed, rstd, grad):
    return rstd * (
        grad
        - jnp.mean(grad, axis=-1, keepdims=True)
        - normed * jnp.mean(grad * normed, axis=-1, keepdims=True)
    )


def mm(left, right, dims=((1,), (0,))):
    return lax.dot_general(left, right, (dims, ((), ())), preferred_element_type=F32)


NT = ((1,), (1,))
TN = ((0,), (0,))


def block(shape):
    rank = len(shape)
    return pl.BlockSpec((1,) + tuple(shape[1:]), lambda i: (i,) + (0,) * (rank - 1))


def whole(shape):
    rank = len(shape)
    return pl.BlockSpec(tuple(shape), lambda i: (0,) * rank)


def call(body, grid, ins, outs, fixed=0, scratch=()):
    moving = len(outs) - fixed
    return pl.pallas_call(
        body,
        grid=(grid,),
        in_specs=[block(a.shape) if step else whole(a.shape) for a, step in ins],
        out_specs=[block(shape) for shape, _ in outs[:moving]]
        + [whole(shape) for shape, _ in outs[moving:]],
        scratch_shapes=list(scratch),
        out_shape=[jax.ShapeDtypeStruct(shape, dtype) for shape, dtype in outs],
    )(*[a for a, _ in ins])


def gather_body(picks, tokens, cotangent, routed, grad_two):
    slots, patches = routed.shape[1], tokens.shape[1]
    hot = (lax.broadcasted_iota(jnp.int32, (slots, patches), 1) == picks[0]).astype(F32)
    hot = hot.astype(BF16)
    routed[0] = mm(hot, tokens[0]).astype(BF16)
    grad_two[0] = mm(hot, cotangent[0]).astype(BF16)


def mod_row(mod, index):
    return mod[0][index : index + 1, :]


def live_rows(keep, slots):
    return (lax.broadcasted_iota(jnp.int32, (slots, 1), 0).astype(F32) < keep[0][:, :1]).astype(F32)


def live_keys(keep, slots):
    return lax.broadcasted_iota(jnp.int32, (1, slots), 1).astype(F32) < keep[0][:, :1]


def head_mask(head, head_dim, cols):
    lane = lax.broadcasted_iota(jnp.int32, (1, cols), 1)
    inside = jnp.logical_and(lane >= head * head_dim, lane < (head + 1) * head_dim)
    return inside.astype(F32).astype(BF16)


def softmax_of(query, key, alive, scale):
    scores = mm(query, key, NT) * scale
    scores = jnp.where(alive, scores, -1e30)
    raised = jnp.exp(scores - jnp.max(scores, axis=-1, keepdims=True))
    return raised / jnp.sum(raised, axis=-1, keepdims=True)


def attend_body(head_dim, routed, mod, keep, weight, bias, out_weight, mixed, qkv, attended, branch):
    slots, cols = routed.shape[1], weight.shape[1]
    scale = 1.0 / math.sqrt(head_dim)
    normed, _ = norm_rows(routed[0].astype(F32))
    rows = (normed * (1.0 + mod_row(mod, 1)) + mod_row(mod, 0)).astype(BF16)
    mixed[0] = rows
    query = (mm(rows, weight[0], NT) + bias[0:1, :]).astype(BF16)
    key = mm(rows, weight[1], NT).astype(BF16)
    value = (mm(rows, weight[2], NT) + bias[1:2, :]).astype(BF16)
    qkv[0, 0] = query
    qkv[0, 1] = key
    qkv[0, 2] = value
    alive = live_keys(keep, slots)
    total = jnp.zeros((slots, cols), F32)
    for head in range(cols // head_dim):
        mask = head_mask(head, head_dim, cols)
        low = softmax_of(query * mask, key, alive, scale).astype(BF16)
        total = total + mm(low, value * mask)
    total = total.astype(BF16)
    attended[0] = total
    branch[0] = mm(total, out_weight[...]).astype(BF16)


def attend_back_body(
    head_dim, grad, qkv, routed, mixed, attended, keep, weight, out_weight,
    mixed_grad, stats, bias_sums, part, total,
):
    slots, cols = routed.shape[1], weight.shape[1]
    scale = 1.0 / math.sqrt(head_dim)
    rows_grad = grad[0]
    attended_grad = mm(rows_grad, out_weight[...], NT).astype(BF16)
    query, key, value = qkv[0, 0], qkv[0, 1], qkv[0, 2]
    alive = live_keys(keep, slots)
    query_grad = jnp.zeros((slots, cols), F32)
    key_grad = jnp.zeros((slots, cols), F32)
    value_grad = jnp.zeros((slots, cols), F32)
    for head in range(cols // head_dim):
        mask = head_mask(head, head_dim, cols)
        own_query = query * mask
        weights = softmax_of(own_query, key, alive, scale)
        own_grad = attended_grad * mask
        weight_grad = mm(own_grad, value, NT)
        value_grad = value_grad + mm(weights.astype(BF16), own_grad, TN)
        row_total = jnp.sum(weights * weight_grad, axis=-1, keepdims=True)
        score_grad = (weights * (weight_grad - row_total)).astype(BF16)
        query_grad = query_grad + mm(score_grad, key * mask)
        key_grad = key_grad + mm(score_grad, own_query, TN)
    query_grad = (query_grad * scale).astype(BF16)
    key_grad = (key_grad * scale).astype(BF16)
    value_grad = value_grad.astype(BF16)
    step = pl.program_id(0)

    @pl.when(step == 0)
    def _():
        total[...] = jnp.zeros_like(total)

    total[0] += mm(query_grad, mixed[0], TN)
    total[1] += mm(key_grad, mixed[0], TN)
    total[2] += mm(value_grad, mixed[0], TN)
    total[3] += mm(attended[0], rows_grad, TN)

    @pl.when(step == pl.num_programs(0) - 1)
    def _():
        part[...] = total[...].astype(BF16)

    rows = mm(query_grad, weight[0]) + mm(key_grad, weight[1]) + mm(value_grad, weight[2])
    mixed_grad[0] = rows.astype(BF16)
    normed, _ = norm_rows(routed[0].astype(F32))
    stats[0, 0:1, :] = jnp.sum(rows, axis=0, keepdims=True)
    stats[0, 1:2, :] = jnp.sum(rows * normed, axis=0, keepdims=True)
    stats[0, 2:3, :] = jnp.sum(rows_grad.astype(F32), axis=0, keepdims=True)
    bias_sums[0, 0:1, :] = jnp.sum(query_grad.astype(F32), axis=0, keepdims=True)
    bias_sums[0, 1:2, :] = jnp.sum(value_grad.astype(F32), axis=0, keepdims=True)


def down_back_body(grad_two, mod, keep, down, down_grad, active_grad, down_sum):
    gate = live_rows(keep, grad_two.shape[1]) * mod_row(mod, 5)
    rows = (gate * grad_two[0].astype(F32)).astype(BF16)
    down_grad[0] = rows
    down_sum[0] = jnp.sum(rows.astype(F32), axis=0, keepdims=True)
    active_grad[0] = mm(rows, down[...], NT)


def forward_body(mixed, active_grad, up, up_bias, active, before_grad, mixed_grad, up_sum):
    units = up.shape[0]
    step = 384 if units % 384 == 0 else units
    rows = mixed[0]
    total = None
    for start in range(0, units, step):
        at = slice(start, start + step)
        before = mm(rows, up[at, :], NT) + up_bias[:, at]
        square = before * before
        tanh = jnp.tanh(GELU_A * (before + GELU_B * (before * square)))
        half = 0.5 * (1.0 + tanh)
        active[0, :, at] = (before * half).astype(BF16)
        slope = half + 0.5 * before * (1.0 - tanh * tanh) * (
            GELU_A * (1.0 + 3.0 * GELU_B * square)
        )
        inner = (active_grad[0, :, at] * slope).astype(BF16)
        before_grad[0, :, at] = inner
        up_sum[0, :, at] = jnp.sum(inner.astype(F32), axis=0, keepdims=True)
        piece = mm(inner, up[at, :])
        total = piece if total is None else total + piece
    mixed_grad[0] = total.astype(BF16)


def branch_body(active, grad_two, keep, down, bias, branch, gate_grad):
    rows = mm(active[0], down[...])
    branch[0] = rows.astype(BF16)
    grad = live_rows(keep, grad_two.shape[1]) * grad_two[0].astype(F32)
    gate_grad[0] = jnp.sum(grad * (rows + bias[...]), axis=0, keepdims=True)


def middle_body(branch, out_bias, routed, mod, keep, hidden, mixed):
    slots = routed.shape[1]
    branch_one = branch[0].astype(F32) + out_bias[...]
    rows = routed[0].astype(F32) + live_rows(keep, slots) * mod_row(mod, 2) * branch_one
    hidden[0] = rows
    normed, _ = norm_rows(rows)
    mixed[0] = (normed * (1.0 + mod_row(mod, 4)) + mod_row(mod, 3)).astype(BF16)


def middle_back_body(
    mixed_grad, hidden, branch, out_bias, grad_two, mod, keep, grad_one, branch_grad, stats
):
    slots = hidden.shape[1]
    rows = mixed_grad[0].astype(F32)
    normed, rstd = norm_rows(hidden[0])
    grad = grad_two[0].astype(F32) + norm_back(normed, rstd, rows * (1.0 + mod_row(mod, 4)))
    grad_one[0] = grad
    live = live_rows(keep, slots)
    branch_one = branch[0].astype(F32) + out_bias[...]
    stats[0, 0:1, :] = jnp.sum(live * grad * branch_one, axis=0, keepdims=True)
    stats[0, 1:2, :] = jnp.sum(rows, axis=0, keepdims=True)
    stats[0, 2:3, :] = jnp.sum(rows * normed, axis=0, keepdims=True)
    branch_grad[0] = (live * mod_row(mod, 2) * grad).astype(BF16)


def place(picks, base, rows):
    patches, slots = base.shape[0], rows.shape[0]
    hot = (lax.broadcasted_iota(jnp.int32, (patches, slots), 0) == picks).astype(F32)
    taken = jnp.max(hot, axis=1, keepdims=True) > 0
    return jnp.where(taken, mm(hot.astype(BF16), rows.astype(BF16)), base.astype(F32)).astype(BF16)


def out_body(branch, hidden, down_bias, mod, keep, picks, tokens, layer_out):
    branch_two = branch[0].astype(F32) + down_bias[...]
    rows = hidden[0] + live_rows(keep, hidden.shape[1]) * mod_row(mod, 5) * branch_two
    layer_out[0] = place(picks[0], tokens[0], rows)


def first_back_body(mixed_grad, routed, mod, grad_one, picks, cotangent, tokens_grad):
    normed, rstd = norm_rows(routed[0].astype(F32))
    rows = mixed_grad[0].astype(F32) * (1.0 + mod_row(mod, 1))
    tokens_grad[0] = place(picks[0], cotangent[0], grad_one[0] + norm_back(normed, rstd, rows))


def dp_bits():
    count = lax.axis_size("dp").bit_length() - 1
    return list(range(count))


def partner(bit):
    return [(i, i ^ (1 << bit)) for i in range(lax.axis_size("dp"))]


def halve(part, bit):
    side = (lax.axis_index("dp") >> bit) & 1
    halves = part.reshape(2, part.shape[0] // 2, part.shape[1])
    own = lax.dynamic_index_in_dim(halves, side, 0, keepdims=False)
    other = lax.dynamic_index_in_dim(halves, 1 - side, 0, keepdims=False)
    return own, lax.ppermute(other, "dp", partner(bit))


def add_low(own, got):
    return (own.astype(F32) + got.astype(F32)).astype(BF16)


def double(part, bit):
    return part, lax.ppermute(part, "dp", partner(bit))


def join(own, got, bit):
    side = (lax.axis_index("dp") >> bit) & 1
    return jnp.where(side == 0, jnp.concatenate([own, got], 0), jnp.concatenate([got, own], 0))


def after(value, *others):
    return lax.optimization_barrier((value,) + others)[0]


def halve_all(parts, level):
    ways = orders()
    flights = [halve(part, way[level]) for part, way in zip(parts, ways)]
    return [add_low(own, got) for own, got in lax.optimization_barrier(flights)]


def double_all(parts, level):
    flights = [double(part, way[level]) for part, way in zip(parts, orders())]
    return lax.optimization_barrier(flights)


def join_all(flights, level):
    return [join(own, got, way[level]) for (own, got), way in zip(flights, orders())]


def trade(part):
    count, mine = lax.axis_size("dp") // 2, lax.axis_index("dp") >> 1
    blocks = part.reshape(count, part.shape[0] // count, part.shape[1])
    own = lax.dynamic_index_in_dim(blocks, mine, 0, keepdims=False)
    sends = [
        lax.dynamic_index_in_dim(blocks, mine ^ step, 0, keepdims=False) for step in range(1, count)
    ]
    return [own] + far(sends)


def far(sends):
    every = range(lax.axis_size("dp"))
    return [
        lax.ppermute(send, "dp", [(i, i ^ (2 * step)) for i in every])
        for step, send in enumerate(sends, 1)
    ]


def spread(block):
    return [block] + far([block] * (lax.axis_size("dp") // 2 - 1))


def finish_body(places, own, got, first, second):
    count, rows = own.shape[0], first.shape[1]
    cut = first.shape[0]
    side, mine = places[0], places[1]

    def block(step):
        place = (step % count) ^ mine
        left, right = own[place, :rows, :], got[place, :rows, :]
        return jnp.where(step // count == side, left, right).astype(F32)

    def fill_first(step, carry):
        first[step] = block(step)
        return carry

    def fill_second(step, carry):
        second[step] = block(step + cut)
        return carry

    lax.fori_loop(0, cut, fill_first, 0)
    lax.fori_loop(0, 2 * count - cut, fill_second, 0)


def finish(own, got, rows):
    count, _, width = own.shape
    index = lax.axis_index("dp")
    places = jnp.stack([index & 1, index >> 1]).astype(jnp.int32)
    cut = 3 * count // 2
    vmem = pl.BlockSpec(memory_space=pltpu.VMEM)
    return pl.pallas_call(
        finish_body,
        in_specs=[pl.BlockSpec(memory_space=pltpu.SMEM), vmem, vmem],
        out_specs=[vmem, vmem],
        out_shape=[
            jax.ShapeDtypeStruct((cut, rows, width), F32),
            jax.ShapeDtypeStruct((2 * count - cut, rows, width), F32),
        ],
        name="finish",
    )(places, own, got)


def orders():
    bits = dp_bits()
    return bits, bits[:1] + bits[2:] + bits[1:2]


def shift(value, step):
    count = lax.axis_size("mp")
    return lax.ppermute(value, "mp", [(i, (i + step) % count) for i in range(count)])


def small_gather(value):
    count, here = lax.axis_size("mp"), lax.axis_index("mp")
    rows = jnp.stack([value] + [shift(value, step) for step in range(1, count)])
    return jnp.take(rows, (here - jnp.arange(count)) % count, axis=0)


def small_scatter_sum(parts):
    count, here = lax.axis_size("mp"), lax.axis_index("mp")
    total = lax.dynamic_index_in_dim(parts, here, 0, keepdims=False)
    for step in range(1, count):
        to = (here + step) % count
        total = total + shift(lax.dynamic_index_in_dim(parts, to, 0, keepdims=False), step)
    return total


def all_rows(rows):
    return lax.all_gather(rows, "mp", axis=0, tiled=True)


def chain_rows(rows):
    count = lax.axis_size("mp")
    up = down = rows
    ups, downs = [], []
    for hop in range(1, count):
        up = lax.ppermute(up, "mp", [(i, i + 1) for i in range(hop - 1, count - 1)])
        down = lax.ppermute(down, "mp", [(i, i - 1) for i in range(count - hop, 0, -1)])
        ups.append(up)
        downs.append(down)
    return ups, downs


def in_order(rows, ups, downs):
    count, here = lax.axis_size("mp"), lax.axis_index("mp")
    slots = [rows] + [
        jnp.where(here > hop, up, down) for hop, (up, down) in enumerate(zip(ups, downs[::-1]))
    ]
    order = (here - jnp.arange(count)) % count
    return jnp.concatenate(
        [lax.dynamic_index_in_dim(jnp.stack(slots), order[i], 0, False) for i in range(count)]
    )


def own_sum(rows):
    return lax.psum_scatter(rows, "mp", scatter_dimension=0, tiled=True)


def per_device(
    tokens, conditioning, routes, keep_count, cotangent, ada_weight, ada_bias, qkv_weight,
    qv_bias, out_weight, out_bias, up_weight, up_bias, down_weight, down_bias,
):
    images = conditioning.shape[0]
    width = tokens.shape[1]
    patches = routes.shape[1]
    slots = 3 * patches // 4
    cols = qkv_weight.shape[1]
    head_dim = width // HEADS
    hidden_units = up_weight.shape[0]
    members = lax.axis_size("mp")
    groups = lax.axis_size("dp")
    group = members * images
    here = lax.axis_index("mp")

    image_tokens = tokens.reshape(images, patches, width)
    image_cot = cotangent.reshape(images, patches, width)
    picks = routes[:, :slots]
    picks_col = picks.reshape(images, slots, 1)
    picks_row = picks.reshape(images, 1, slots)
    rows_shape = (images, slots, width)
    group_shape = (group, slots, width)

    routed, grad_two = call(
        gather_body, images,
        [(picks_col, True), (image_tokens, True), (image_cot, True)],
        [(rows_shape, BF16), (rows_shape, BF16)],
    )
    group_routed = all_rows(routed)
    near = members <= 4
    if near:
        hops = chain_rows(after(grad_two, group_routed))
    else:
        group_two = all_rows(grad_two)

    small = jnp.concatenate(
        [conditioning, jnp.broadcast_to(keep_count.astype(BF16)[:, None], (images, 128))], axis=1
    )
    small = small_gather(small).reshape(group, width + 128)
    silu_cond = jax.nn.silu(small[:, :width].astype(F32)).astype(BF16)
    modulation = mm(silu_cond, ada_weight, NT) + ada_bias.astype(F32)
    modulation = modulation.reshape(group, 6, width)
    keep = small[:, None, width:].astype(F32)
    own_mod = lax.dynamic_slice_in_dim(modulation, here * images, images, 0)
    own_keep = jnp.broadcast_to(keep_count.astype(F32)[:, None, None], (images, 1, 128))
    out_bias_row = out_bias.astype(F32)[None]
    down_bias_row = down_bias.astype(F32)[None]

    mixed_one, qkv, attended, branch = call(
        functools.partial(attend_body, head_dim), group,
        [
            (group_routed, True), (modulation, True), (keep, True), (qkv_weight, False),
            (qv_bias.astype(F32), False), (out_weight, False),
        ],
        [
            (group_shape, BF16), ((group, 3, slots, cols), BF16), ((group, slots, cols), BF16),
            (group_shape, BF16),
        ],
    )
    branch_one = own_sum(branch)
    hidden_one, mixed_two = call(
        middle_body, images,
        [
            (branch_one, True), (out_bias_row, False), (routed, True), (own_mod, True),
            (own_keep, True),
        ],
        [(rows_shape, F32), (rows_shape, BF16)],
    )
    group_mixed = all_rows(mixed_two)
    if near:
        group_two = in_order(grad_two, *after(hops, mixed_two))
    unit_shape = (group, slots, hidden_units)
    down_grad, active_grad, down_sum = call(
        down_back_body, group,
        [(group_two, True), (modulation, True), (keep, True), (down_weight, False)],
        [(group_shape, BF16), (unit_shape, F32), ((group, 1, width), F32)],
    )
    active, before_grad, mixed_grad, up_sum = call(
        forward_body, group,
        [
            (group_mixed, True), (active_grad, True), (up_weight, False),
            (up_bias.astype(F32)[None], False),
        ],
        [
            (unit_shape, BF16), (unit_shape, BF16), (group_shape, BF16),
            ((group, 1, hidden_units), F32),
        ],
    )
    mixed_two_grad = own_sum(mixed_grad)
    flat = (group * slots, hidden_units)
    wide = (group * slots, width)
    up_part = mm(before_grad.reshape(flat), group_mixed.reshape(wide), TN).astype(BF16)
    down_part = mm(active.reshape(flat), down_grad.reshape(wide), TN).astype(BF16)
    levels = len(dp_bits())
    sums = halve_all((up_part, down_part), 0)
    branch, gate_grad = call(
        branch_body, group,
        [
            (active, True), (group_two, True), (after(keep, *sums), True), (down_weight, False),
            (jnp.where(here == 0, down_bias_row, 0.0), False),
        ],
        [(group_shape, BF16), ((group, 1, width), F32)],
    )
    sums = halve_all(sums, 1)

    grad_one, branch_grad, middle_stats = call(
        middle_back_body, images,
        [
            (mixed_two_grad, True), (hidden_one, True), (branch_one, True), (out_bias_row, False),
            (grad_two, True), (own_mod, True), (after(own_keep, gate_grad), True),
        ],
        [(rows_shape, F32), (rows_shape, BF16), ((images, 3, width), F32)],
    )
    group_grad = all_rows(branch_grad)
    branch_two = own_sum(branch)
    for level in range(2, levels):
        sums = halve_all(sums, level)
    for level in reversed(range(1, levels)):
        sums = join_all(double_all(sums, level), level)
    last = double_all(sums, 0)
    mixed_grad, attend_stats, bias_sums, part = call(
        functools.partial(attend_back_body, head_dim), group,
        [
            (group_grad, True), (qkv, True), (group_routed, True), (mixed_one, True),
            (attended, True), (after(keep, last), True),
            (qkv_weight, False), (out_weight, False),
        ],
        [
            (group_shape, BF16), ((group, 3, width), F32), ((group, 2, cols), F32),
            ((4, cols, width), BF16),
        ],
        fixed=1,
        scratch=[pltpu.VMEM((4, cols, width), F32)],
    )
    (layer_out,) = call(
        out_body, images,
        [
            (branch_two, True), (hidden_one, True), (down_bias_row, False), (own_mod, True),
            (after(own_keep, attend_stats), True), (picks_row, True), (image_tokens, True),
        ],
        [((images, patches, width), BF16)],
    )
    mixed_one_grad = own_sum(mixed_grad)
    half = add_low(*halve(part.reshape(4 * cols, width), 0))
    last = after(last, half)
    blocks = trade(half)

    placed = lax.dynamic_update_slice(
        jnp.zeros((group, 3, width), F32), middle_stats, (here * images, 0, 0)
    )
    mod_grad = jnp.concatenate([attend_stats[:, :2], placed, gate_grad], axis=1)
    each = 6 * width // (groups * members)
    mod_grad = mod_grad.reshape(group, groups, members, each)
    mod_grad = small_scatter_sum(mod_grad.transpose(2, 0, 1, 3)).astype(BF16)
    pieces = [
        mod_grad.reshape(-1),
        silu_cond.reshape(-1),
        jnp.sum(bias_sums, axis=0).astype(BF16).reshape(-1),
        jnp.sum(attend_stats[:, 2], axis=0).astype(BF16),
        jnp.sum(up_sum, axis=0).astype(BF16).reshape(-1),
        jnp.sum(down_sum, axis=0).astype(BF16).reshape(-1),
    ]
    sizes = [piece.shape[0] for piece in pieces]
    packed = jnp.concatenate(pieces)
    packed = jnp.pad(packed, (0, -packed.shape[0] % (16 * width))).reshape(-1, width)
    blocks = after(blocks, packed)
    block_sum = sum(one.astype(F32) for one in blocks).astype(BF16)
    rows = block_sum.shape[0]
    last = after(last, block_sum)
    up_weight_grad, down_weight_grad = [one.astype(F32) for one in join_all(last, 0)]
    pieces = spread(jnp.concatenate([block_sum, packed]))
    own = jnp.stack(after(pieces, up_weight_grad, down_weight_grad, layer_out))
    own, got = double(own, 0)
    qkv_weight_grad, out_weight_grad = finish(own, got, rows)
    qkv_weight_grad = qkv_weight_grad.reshape(3, cols, width)
    out_weight_grad = out_weight_grad.reshape(cols, width)

    packed = jnp.stack([own[:, rows:], got[:, rows:]]).reshape(2, groups // 2, -1)
    place = lax.axis_index("dp")
    order = jnp.arange(groups) ^ place
    packed = packed[order & 1, order >> 1]
    starts = [sum(sizes[:i]) for i in range(len(sizes))]
    views = [packed[:, s : s + n] for s, n in zip(starts, sizes)]
    mod_all = views[0].reshape(groups, group, groups, each)
    mod_all = lax.dynamic_index_in_dim(mod_all, lax.axis_index("dp"), 2, keepdims=False)
    mod_all = mod_all.reshape(groups * group, each)
    cond_all = views[1].reshape(groups * group, width)
    ada_weight_grad = mm(mod_all, cond_all, TN)
    ada_bias_grad = jnp.sum(mod_all.astype(F32), axis=0)
    qv_sum, out_sum, up_bias_grad, down_bias_grad = [
        jnp.sum(view.astype(F32), axis=0) for view in views[2:]
    ]

    tokens_grad = call(
        first_back_body, images,
        [
            (mixed_one_grad, True), (routed, True), (own_mod, True), (grad_one, True),
            (after(picks_row, ada_weight_grad), True), (image_cot, True),
        ],
        [((images, patches, width), BF16)],
    )[0]
    return (
        layer_out.reshape(images * patches, width),
        tokens_grad.reshape(images * patches, width),
        ada_weight_grad,
        ada_bias_grad,
        qkv_weight_grad,
        qv_sum.reshape(2, cols),
        out_weight_grad,
        out_sum,
        up_weight_grad,
        up_bias_grad,
        down_weight_grad,
        down_bias_grad,
    )


def solution(mesh):
    both = ("dp", "mp")
    in_specs = (
        P(both, None), P(both, None), P(both, None), P(both), P(both, None), P(), P(),
        P(None, "mp", None), P(None, "mp"), P("mp", None), P(), P("mp", None), P("mp"),
        P("mp", None), P(),
    )
    out_specs = (
        P(both, None), P(both, None), P(both, None), P(both), P(None, "mp", None), P(None, "mp"),
        P("mp", None), P(), P("mp", None), P("mp"), P("mp", None), P(),
    )

    return jax.shard_map(
        per_device, mesh=mesh, in_specs=in_specs, out_specs=out_specs, check_vma=False
    )
```

```python
import functools
import math

import jax
import jax.numpy as jnp
from jax import lax
from jax.experimental import pallas as pl
from jax.experimental.pallas import tpu as pltpu
from jax.sharding import PartitionSpec as P


HEADS = 16
EPS = 1e-06
F32 = jnp.float32
BF16 = jnp.bfloat16
GELU_A = math.sqrt(2.0 / math.pi)
GELU_B = 0.044715


def norm_rows(rows):
    mean = jnp.mean(rows, axis=-1, keepdims=True)
    centred = rows - mean
    rstd = lax.rsqrt(jnp.mean(centred * centred, axis=-1, keepdims=True) + EPS)
    return centred * rstd, rstd


def norm_back(normed, rstd, grad):
    return rstd * (
        grad
        - jnp.mean(grad, axis=-1, keepdims=True)
        - normed * jnp.mean(grad * normed, axis=-1, keepdims=True)
    )


def mm(left, right, dims=((1,), (0,))):
    return lax.dot_general(left, right, (dims, ((), ())), preferred_element_type=F32)


NT = ((1,), (1,))
TN = ((0,), (0,))


def block(shape):
    rank = len(shape)
    return pl.BlockSpec((1,) + tuple(shape[1:]), lambda i: (i,) + (0,) * (rank - 1))


def whole(shape):
    rank = len(shape)
    return pl.BlockSpec(tuple(shape), lambda i: (0,) * rank)


def call(body, grid, ins, outs, fixed=0, scratch=()):
    moving = len(outs) - fixed
    return pl.pallas_call(
        body,
        grid=(grid,),
        in_specs=[block(a.shape) if step else whole(a.shape) for a, step in ins],
        out_specs=[block(shape) for shape, _ in outs[:moving]]
        + [whole(shape) for shape, _ in outs[moving:]],
        scratch_shapes=list(scratch),
        out_shape=[jax.ShapeDtypeStruct(shape, dtype) for shape, dtype in outs],
    )(*[a for a, _ in ins])


def split_call(body, start, images, group, own_ins, group_ins, outs, fixed=(), scratch=()):
    start = jnp.full((1,), start, jnp.int32)
    shapes = [jax.ShapeDtypeStruct(shape, dtype) for shape, dtype in outs]
    apart = [jax.ShapeDtypeStruct(shape, dtype) for shape, dtype in fixed]

    def at(shape, first, moving):
        rest = (0,) * (len(shape) - 1)

        def place(i, p):
            return ((p[0] + first + i) % group if moving else i,) + rest

        return pl.BlockSpec((1,) + tuple(shape[1:]), place)

    def full(shape):
        return pl.BlockSpec(tuple(shape), lambda i, p: (0,) * len(shape))

    def run(ins, first, count, filled, moving):
        def step(index, *refs):
            body(*refs[: len(ins)], *refs[len(ins) + len(filled) :])

        return pl.pallas_call(
            step,
            grid_spec=pltpu.PrefetchScalarGridSpec(
                num_scalar_prefetch=1,
                grid=(count,),
                in_specs=[at(a.shape, first, moving) if by else full(a.shape) for a, by in ins]
                + [pl.BlockSpec(memory_space=pl.ANY)] * len(filled),
                out_specs=[at(one.shape, first, True) for one in shapes]
                + [full(one.shape) for one in apart],
                scratch_shapes=list(scratch),
            ),
            out_shape=shapes + apart,
            input_output_aliases={1 + len(ins) + i: i for i in range(len(filled))},
        )(start, *[a for a, _ in ins], *filled)

    own = run(own_ins, 0, images, [], False)
    rest = run(group_ins, images, group - images, own[: len(shapes)], True)
    return list(rest[: len(shapes)]) + [(a, b) for a, b in zip(own[len(shapes) :], rest[len(shapes) :])]


def gather_body(picks, tokens, cotangent, routed, grad_two):
    slots, patches = routed.shape[1], tokens.shape[1]
    hot = (lax.broadcasted_iota(jnp.int32, (slots, patches), 1) == picks[0]).astype(F32)
    hot = hot.astype(BF16)
    routed[0] = mm(hot, tokens[0]).astype(BF16)
    grad_two[0] = mm(hot, cotangent[0]).astype(BF16)


def mod_row(mod, index):
    return mod[0][index : index + 1, :]


def live_rows(keep, slots):
    return (lax.broadcasted_iota(jnp.int32, (slots, 1), 0).astype(F32) < keep[0][:, :1]).astype(F32)


def live_keys(keep, slots):
    return lax.broadcasted_iota(jnp.int32, (1, slots), 1).astype(F32) < keep[0][:, :1]


def head_mask(head, head_dim, cols):
    lane = lax.broadcasted_iota(jnp.int32, (1, cols), 1)
    inside = jnp.logical_and(lane >= head * head_dim, lane < (head + 1) * head_dim)
    return inside.astype(F32).astype(BF16)


def softmax_of(query, key, alive, scale):
    scores = mm(query, key, NT) * scale
    scores = jnp.where(alive, scores, -1e30)
    raised = jnp.exp(scores - jnp.max(scores, axis=-1, keepdims=True))
    return raised / jnp.sum(raised, axis=-1, keepdims=True)


def attend_body(head_dim, routed, mod, keep, weight, bias, out_weight, mixed, qkv, attended, branch):
    slots, cols = routed.shape[1], weight.shape[1]
    scale = 1.0 / math.sqrt(head_dim)
    normed, _ = norm_rows(routed[0].astype(F32))
    rows = (normed * (1.0 + mod_row(mod, 1)) + mod_row(mod, 0)).astype(BF16)
    mixed[0] = rows
    query = (mm(rows, weight[0], NT) + bias[0:1, :]).astype(BF16)
    key = mm(rows, weight[1], NT).astype(BF16)
    value = (mm(rows, weight[2], NT) + bias[1:2, :]).astype(BF16)
    qkv[0, 0] = query
    qkv[0, 1] = key
    qkv[0, 2] = value
    alive = live_keys(keep, slots)
    total = jnp.zeros((slots, cols), F32)
    for head in range(cols // head_dim):
        mask = head_mask(head, head_dim, cols)
        low = softmax_of(query * mask, key, alive, scale).astype(BF16)
        total = total + mm(low, value * mask)
    total = total.astype(BF16)
    attended[0] = total
    branch[0] = mm(total, out_weight[...]).astype(BF16)


def attend_back_body(
    head_dim, grad, qkv, routed, mixed, attended, keep, weight, out_weight,
    mixed_grad, stats, bias_sums, part, kept,
):
    slots, cols = routed.shape[1], weight.shape[1]
    scale = 1.0 / math.sqrt(head_dim)
    here = pl.ds(pl.multiple_of(pl.program_id(0) * slots, slots), slots)
    rows_grad = grad[here, :]
    attended_grad = mm(rows_grad, out_weight[...], NT).astype(BF16)
    query, key, value = qkv[0, 0], qkv[0, 1], qkv[0, 2]
    alive = live_keys(keep, slots)
    query_grad = jnp.zeros((slots, cols), F32)
    key_grad = jnp.zeros((slots, cols), F32)
    value_grad = jnp.zeros((slots, cols), F32)
    for head in range(cols // head_dim):
        mask = head_mask(head, head_dim, cols)
        own_query = query * mask
        weights = softmax_of(own_query, key, alive, scale)
        own_grad = attended_grad * mask
        weight_grad = mm(own_grad, value, NT)
        value_grad = value_grad + mm(weights.astype(BF16), own_grad, TN)
        row_total = jnp.sum(weights * weight_grad, axis=-1, keepdims=True)
        score_grad = (weights * (weight_grad - row_total)).astype(BF16)
        query_grad = query_grad + mm(score_grad, key * mask)
        key_grad = key_grad + mm(score_grad, own_query, TN)
    query_grad = (query_grad * scale).astype(BF16)
    key_grad = (key_grad * scale).astype(BF16)
    value_grad = value_grad.astype(BF16)
    for index, one in enumerate((query_grad, key_grad, value_grad)):
        kept[index, here, :] = one
    rows = mm(query_grad, weight[0]) + mm(key_grad, weight[1]) + mm(value_grad, weight[2])
    mixed_grad[0] = rows.astype(BF16)
    normed, _ = norm_rows(routed[0].astype(F32))
    stats[0, 0:1, :] = jnp.sum(rows, axis=0, keepdims=True)
    stats[0, 1:2, :] = jnp.sum(rows * normed, axis=0, keepdims=True)
    stats[0, 2:3, :] = jnp.sum(rows_grad.astype(F32), axis=0, keepdims=True)
    bias_sums[0, 0:1, :] = jnp.sum(query_grad.astype(F32), axis=0, keepdims=True)
    bias_sums[0, 1:2, :] = jnp.sum(value_grad.astype(F32), axis=0, keepdims=True)

    @pl.when(pl.program_id(0) == pl.num_programs(0) - 1)
    def _():
        for index in range(3):
            part[index] = mm(kept[index], mixed[...], TN).astype(BF16)
        part[3] = mm(attended[...], grad[...], TN).astype(BF16)


def down_back_body(grad_two, mod, keep, down, down_grad, active_grad, down_sum):
    gate = live_rows(keep, grad_two.shape[1]) * mod_row(mod, 5)
    rows = (gate * grad_two[0].astype(F32)).astype(BF16)
    down_grad[0] = rows
    down_sum[0] = jnp.sum(rows.astype(F32), axis=0, keepdims=True)
    active_grad[0] = mm(rows, down[...], NT)


def forward_body(mixed, active_grad, up, up_bias, active, before_grad, mixed_grad, up_sum):
    units = up.shape[0]
    step = 384 if units % 384 == 0 else units
    rows = mixed[0]
    total = None
    for start in range(0, units, step):
        at = slice(start, start + step)
        before = mm(rows, up[at, :], NT) + up_bias[:, at]
        square = before * before
        tanh = jnp.tanh(GELU_A * (before + GELU_B * (before * square)))
        half = 0.5 * (1.0 + tanh)
        active[0, :, at] = (before * half).astype(BF16)
        slope = half + 0.5 * before * (1.0 - tanh * tanh) * (
            GELU_A * (1.0 + 3.0 * GELU_B * square)
        )
        inner = (active_grad[0, :, at] * slope).astype(BF16)
        before_grad[0, :, at] = inner
        up_sum[0, :, at] = jnp.sum(inner.astype(F32), axis=0, keepdims=True)
        piece = mm(inner, up[at, :])
        total = piece if total is None else total + piece
    mixed_grad[0] = total.astype(BF16)


def branch_body(active, grad_two, keep, down, bias, branch, gate_grad):
    rows = mm(active[0], down[...])
    branch[0] = rows.astype(BF16)
    grad = live_rows(keep, grad_two.shape[1]) * grad_two[0].astype(F32)
    gate_grad[0] = jnp.sum(grad * (rows + bias[...]), axis=0, keepdims=True)


def middle_body(branch, out_bias, routed, mod, keep, hidden, mixed):
    slots = routed.shape[1]
    branch_one = branch[0].astype(F32) + out_bias[...]
    rows = routed[0].astype(F32) + live_rows(keep, slots) * mod_row(mod, 2) * branch_one
    hidden[0] = rows
    normed, _ = norm_rows(rows)
    mixed[0] = (normed * (1.0 + mod_row(mod, 4)) + mod_row(mod, 3)).astype(BF16)


def middle_back_body(
    mixed_grad, hidden, branch, out_bias, grad_two, mod, keep, grad_one, branch_grad, stats
):
    slots = hidden.shape[1]
    rows = mixed_grad[0].astype(F32)
    normed, rstd = norm_rows(hidden[0])
    grad = grad_two[0].astype(F32) + norm_back(normed, rstd, rows * (1.0 + mod_row(mod, 4)))
    grad_one[0] = grad
    live = live_rows(keep, slots)
    branch_one = branch[0].astype(F32) + out_bias[...]
    stats[0, 0:1, :] = jnp.sum(live * grad * branch_one, axis=0, keepdims=True)
    stats[0, 1:2, :] = jnp.sum(rows, axis=0, keepdims=True)
    stats[0, 2:3, :] = jnp.sum(rows * normed, axis=0, keepdims=True)
    branch_grad[0] = (live * mod_row(mod, 2) * grad).astype(BF16)


def place(picks, base, rows):
    patches, slots = base.shape[0], rows.shape[0]
    hot = (lax.broadcasted_iota(jnp.int32, (patches, slots), 0) == picks).astype(F32)
    taken = jnp.max(hot, axis=1, keepdims=True) > 0
    return jnp.where(taken, mm(hot.astype(BF16), rows.astype(BF16)), base.astype(F32)).astype(BF16)


def out_body(branch, hidden, down_bias, mod, keep, picks, tokens, layer_out):
    branch_two = branch[0].astype(F32) + down_bias[...]
    rows = hidden[0] + live_rows(keep, hidden.shape[1]) * mod_row(mod, 5) * branch_two
    layer_out[0] = place(picks[0], tokens[0], rows)


def first_back_body(mixed_grad, routed, mod, grad_one, picks, cotangent, tokens_grad):
    normed, rstd = norm_rows(routed[0].astype(F32))
    rows = mixed_grad[0].astype(F32) * (1.0 + mod_row(mod, 1))
    tokens_grad[0] = place(picks[0], cotangent[0], grad_one[0] + norm_back(normed, rstd, rows))


def dp_bits():
    count = lax.axis_size("dp").bit_length() - 1
    return list(range(count))


def partner(bit):
    return [(i, i ^ (1 << bit)) for i in range(lax.axis_size("dp"))]


def halve(part, bit):
    side = (lax.axis_index("dp") >> bit) & 1
    halves = part.reshape(2, part.shape[0] // 2, part.shape[1])
    own = lax.dynamic_index_in_dim(halves, side, 0, keepdims=False)
    other = lax.dynamic_index_in_dim(halves, 1 - side, 0, keepdims=False)
    return own, lax.ppermute(other, "dp", partner(bit))


def add_low(own, got):
    return (own.astype(F32) + got.astype(F32)).astype(BF16)


def double(part, bit):
    return part, lax.ppermute(part, "dp", partner(bit))


def join(own, got, bit):
    side = (lax.axis_index("dp") >> bit) & 1
    return jnp.where(side == 0, jnp.concatenate([own, got], 0), jnp.concatenate([got, own], 0))


def after(value, *others):
    return lax.optimization_barrier((value,) + others)[0]


def halve_all(parts, level):
    ways = orders()
    flights = [halve(part, way[level]) for part, way in zip(parts, ways)]
    return [add_low(own, got) for own, got in lax.optimization_barrier(flights)]


def double_all(parts, level):
    flights = [double(part, way[level]) for part, way in zip(parts, orders())]
    return lax.optimization_barrier(flights)


def join_all(flights, level):
    return [join(own, got, way[level]) for (own, got), way in zip(flights, orders())]


def trade(part):
    count, mine = lax.axis_size("dp") // 2, lax.axis_index("dp") >> 1
    blocks = part.reshape(count, part.shape[0] // count, part.shape[1])
    own = lax.dynamic_index_in_dim(blocks, mine, 0, keepdims=False)
    sends = [
        lax.dynamic_index_in_dim(blocks, mine ^ step, 0, keepdims=False) for step in range(1, count)
    ]
    return [own] + far(sends)


def far(sends):
    every = range(lax.axis_size("dp"))
    return [
        lax.ppermute(send, "dp", [(i, i ^ (2 * step)) for i in every])
        for step, send in enumerate(sends, 1)
    ]


def spread(block):
    return [block] + far([block] * (lax.axis_size("dp") // 2 - 1))


def finish_body(places, own, got, first, second):
    count, rows = own.shape[0], first.shape[1]
    cut = first.shape[0]
    side, mine = places[0], places[1]

    def block(step):
        place = (step % count) ^ mine
        left, right = own[place, :rows, :], got[place, :rows, :]
        return jnp.where(step // count == side, left, right).astype(F32)

    def fill_first(step, carry):
        first[step] = block(step)
        return carry

    def fill_second(step, carry):
        second[step] = block(step + cut)
        return carry

    lax.fori_loop(0, cut, fill_first, 0)
    lax.fori_loop(0, 2 * count - cut, fill_second, 0)


def finish(own, got, rows):
    count, _, width = own.shape
    index = lax.axis_index("dp")
    places = jnp.stack([index & 1, index >> 1]).astype(jnp.int32)
    cut = 3 * count // 2
    vmem = pl.BlockSpec(memory_space=pltpu.VMEM)
    return pl.pallas_call(
        finish_body,
        in_specs=[pl.BlockSpec(memory_space=pltpu.SMEM), vmem, vmem],
        out_specs=[vmem, vmem],
        out_shape=[
            jax.ShapeDtypeStruct((cut, rows, width), F32),
            jax.ShapeDtypeStruct((2 * count - cut, rows, width), F32),
        ],
        name="finish",
    )(places, own, got)


def orders():
    bits = dp_bits()
    return bits, bits[:1] + bits[2:] + bits[1:2]


def shift(value, step):
    count = lax.axis_size("mp")
    return lax.ppermute(value, "mp", [(i, (i + step) % count) for i in range(count)])


def small_gather(value):
    count, here = lax.axis_size("mp"), lax.axis_index("mp")
    rows = jnp.stack([value] + [shift(value, step) for step in range(1, count)])
    return jnp.take(rows, (here - jnp.arange(count)) % count, axis=0)


def small_scatter_sum(parts):
    count, here = lax.axis_size("mp"), lax.axis_index("mp")
    total = lax.dynamic_index_in_dim(parts, here, 0, keepdims=False)
    for step in range(1, count):
        to = (here + step) % count
        total = total + shift(lax.dynamic_index_in_dim(parts, to, 0, keepdims=False), step)
    return total


def all_rows(rows):
    return lax.all_gather(rows, "mp", axis=0, tiled=True)


def chain_rows(rows):
    count = lax.axis_size("mp")
    up = down = rows
    ups, downs = [], []
    for hop in range(1, count):
        up = lax.ppermute(up, "mp", [(i, i + 1) for i in range(hop - 1, count - 1)])
        down = lax.ppermute(down, "mp", [(i, i - 1) for i in range(count - hop, 0, -1)])
        ups.append(up)
        downs.append(down)
    return ups, downs


def in_order(rows, ups, downs):
    count, here = lax.axis_size("mp"), lax.axis_index("mp")
    slots = [rows] + [
        jnp.where(here > hop, up, down) for hop, (up, down) in enumerate(zip(ups, downs[::-1]))
    ]
    order = (here - jnp.arange(count)) % count
    return jnp.concatenate(
        [lax.dynamic_index_in_dim(jnp.stack(slots), order[i], 0, False) for i in range(count)]
    )


def own_sum(rows):
    return lax.psum_scatter(rows, "mp", scatter_dimension=0, tiled=True)


def per_device(
    tokens, conditioning, routes, keep_count, cotangent, ada_weight, ada_bias, qkv_weight,
    qv_bias, out_weight, out_bias, up_weight, up_bias, down_weight, down_bias,
):
    images = conditioning.shape[0]
    width = tokens.shape[1]
    patches = routes.shape[1]
    slots = 3 * patches // 4
    cols = qkv_weight.shape[1]
    head_dim = width // HEADS
    hidden_units = up_weight.shape[0]
    members = lax.axis_size("mp")
    groups = lax.axis_size("dp")
    group = members * images
    here = lax.axis_index("mp")

    image_tokens = tokens.reshape(images, patches, width)
    image_cot = cotangent.reshape(images, patches, width)
    picks = routes[:, :slots]
    picks_col = picks.reshape(images, slots, 1)
    picks_row = picks.reshape(images, 1, slots)
    rows_shape = (images, slots, width)
    group_shape = (group, slots, width)

    routed, grad_two = call(
        gather_body, images,
        [(picks_col, True), (image_tokens, True), (image_cot, True)],
        [(rows_shape, BF16), (rows_shape, BF16)],
    )
    group_routed = all_rows(routed)
    near = members <= 4
    if near:
        hops = chain_rows(after(grad_two, group_routed))
    else:
        group_two = all_rows(grad_two)

    small = jnp.concatenate(
        [conditioning, jnp.broadcast_to(keep_count.astype(BF16)[:, None], (images, 128))], axis=1
    )
    small = small_gather(small).reshape(group, width + 128)
    silu_cond = jax.nn.silu(small[:, :width].astype(F32)).astype(BF16)
    modulation = mm(silu_cond, ada_weight, NT) + ada_bias.astype(F32)
    modulation = modulation.reshape(group, 6, width)
    keep = small[:, None, width:].astype(F32)
    own_mod = lax.dynamic_slice_in_dim(modulation, here * images, images, 0)
    own_keep = jnp.broadcast_to(keep_count.astype(F32)[:, None, None], (images, 1, 128))
    out_bias_row = out_bias.astype(F32)[None]
    down_bias_row = down_bias.astype(F32)[None]

    first_image = here * images
    fixed_ins = [(qkv_weight, False), (qv_bias.astype(F32), False), (out_weight, False)]
    mixed_one, qkv, attended, branch = split_call(
        functools.partial(attend_body, head_dim), first_image, images, group,
        [(routed, True), (own_mod, True), (own_keep, True)] + fixed_ins,
        [(group_routed, True), (modulation, True), (keep, True)] + fixed_ins,
        [
            (group_shape, BF16), ((group, 3, slots, cols), BF16), ((group, slots, cols), BF16),
            (group_shape, BF16),
        ],
    )
    branch_one = own_sum(branch)
    hidden_one, mixed_two = call(
        middle_body, images,
        [
            (branch_one, True), (out_bias_row, False), (routed, True), (own_mod, True),
            (own_keep, True),
        ],
        [(rows_shape, F32), (rows_shape, BF16)],
    )
    group_mixed = all_rows(mixed_two)
    if near:
        group_two = in_order(grad_two, *after(hops, mixed_two))
    unit_shape = (group, slots, hidden_units)
    down_grad, active_grad, down_sum = call(
        down_back_body, group,
        [(group_two, True), (modulation, True), (keep, True), (down_weight, False)],
        [(group_shape, BF16), (unit_shape, F32), ((group, 1, width), F32)],
    )
    own_active_grad = lax.dynamic_slice_in_dim(active_grad, first_image, images, 0)
    fixed_ins = [(up_weight, False), (up_bias.astype(F32)[None], False)]
    active, before_grad, mixed_grad, up_sum = split_call(
        forward_body, first_image, images, group,
        [(mixed_two, True), (own_active_grad, True)] + fixed_ins,
        [(group_mixed, True), (active_grad, True)] + fixed_ins,
        [
            (unit_shape, BF16), (unit_shape, BF16), (group_shape, BF16),
            ((group, 1, hidden_units), F32),
        ],
    )
    mixed_two_grad = own_sum(mixed_grad)
    flat = (group * slots, hidden_units)
    wide = (group * slots, width)
    up_part = mm(before_grad.reshape(flat), group_mixed.reshape(wide), TN).astype(BF16)
    down_part = mm(active.reshape(flat), down_grad.reshape(wide), TN).astype(BF16)
    levels = len(dp_bits())
    sums = halve_all((up_part, down_part), 0)
    branch, gate_grad = call(
        branch_body, group,
        [
            (active, True), (group_two, True), (after(keep, *sums), True), (down_weight, False),
            (jnp.where(here == 0, down_bias_row, 0.0), False),
        ],
        [(group_shape, BF16), ((group, 1, width), F32)],
    )
    sums = halve_all(sums, 1)

    grad_one, branch_grad, middle_stats = call(
        middle_back_body, images,
        [
            (mixed_two_grad, True), (hidden_one, True), (branch_one, True), (out_bias_row, False),
            (grad_two, True), (own_mod, True), (after(own_keep, gate_grad), True),
        ],
        [(rows_shape, F32), (rows_shape, BF16), ((images, 3, width), F32)],
    )
    group_grad = all_rows(branch_grad)
    branch_two = own_sum(branch)
    for level in range(2, levels):
        sums = halve_all(sums, level)
    for level in reversed(range(1, levels)):
        sums = join_all(double_all(sums, level), level)
    last = double_all(sums, 0)
    mixed_grad, attend_stats, bias_sums, part = call(
        functools.partial(attend_back_body, head_dim), group,
        [
            (group_grad.reshape(wide), False), (qkv, True), (group_routed, True),
            (mixed_one.reshape(wide), False), (attended.reshape(-1, cols), False),
            (after(keep, last), True), (qkv_weight, False), (out_weight, False),
        ],
        [
            (group_shape, BF16), ((group, 3, width), F32), ((group, 2, cols), F32),
            ((4, cols, width), BF16),
        ],
        fixed=1,
        scratch=[pltpu.VMEM((3, group * slots, cols), BF16)],
    )
    (layer_out,) = call(
        out_body, images,
        [
            (branch_two, True), (hidden_one, True), (down_bias_row, False), (own_mod, True),
            (after(own_keep, attend_stats), True), (picks_row, True), (image_tokens, True),
        ],
        [((images, patches, width), BF16)],
    )
    mixed_one_grad = own_sum(mixed_grad)
    half = add_low(*halve(part.reshape(4 * cols, width), 0))
    last = after(last, half)
    blocks = trade(half)

    placed = lax.dynamic_update_slice(
        jnp.zeros((group, 3, width), F32), middle_stats, (here * images, 0, 0)
    )
    mod_grad = jnp.concatenate([attend_stats[:, :2], placed, gate_grad], axis=1)
    each = 6 * width // (groups * members)
    mod_grad = mod_grad.reshape(group, groups, members, each)
    mod_grad = small_scatter_sum(mod_grad.transpose(2, 0, 1, 3)).astype(BF16)
    pieces = [
        mod_grad.reshape(-1),
        silu_cond.reshape(-1),
        jnp.sum(bias_sums, axis=0).astype(BF16).reshape(-1),
        jnp.sum(attend_stats[:, 2], axis=0).astype(BF16),
        jnp.sum(up_sum, axis=0).astype(BF16).reshape(-1),
        jnp.sum(down_sum, axis=0).astype(BF16).reshape(-1),
    ]
    sizes = [piece.shape[0] for piece in pieces]
    packed = jnp.concatenate(pieces)
    packed = jnp.pad(packed, (0, -packed.shape[0] % (16 * width))).reshape(-1, width)
    blocks = after(blocks, packed)
    block_sum = sum(one.astype(F32) for one in blocks).astype(BF16)
    rows = block_sum.shape[0]
    last = after(last, block_sum)
    up_weight_grad, down_weight_grad = [one.astype(F32) for one in join_all(last, 0)]
    pieces = spread(jnp.concatenate([block_sum, packed]))
    own = jnp.stack(after(pieces, up_weight_grad, down_weight_grad, layer_out))
    own, got = double(own, 0)
    qkv_weight_grad, out_weight_grad = finish(own, got, rows)
    qkv_weight_grad = qkv_weight_grad.reshape(3, cols, width)
    out_weight_grad = out_weight_grad.reshape(cols, width)

    packed = jnp.stack([own[:, rows:], got[:, rows:]]).reshape(2, groups // 2, -1)
    place = lax.axis_index("dp")
    order = jnp.arange(groups) ^ place
    packed = packed[order & 1, order >> 1]
    starts = [sum(sizes[:i]) for i in range(len(sizes))]
    views = [packed[:, s : s + n] for s, n in zip(starts, sizes)]
    mod_all = views[0].reshape(groups, group, groups, each)
    mod_all = lax.dynamic_index_in_dim(mod_all, lax.axis_index("dp"), 2, keepdims=False)
    mod_all = mod_all.reshape(groups * group, each)
    cond_all = views[1].reshape(groups * group, width)
    ada_weight_grad = mm(mod_all, cond_all, TN)
    ada_bias_grad = jnp.sum(mod_all.astype(F32), axis=0)
    qv_sum, out_sum, up_bias_grad, down_bias_grad = [
        jnp.sum(view.astype(F32), axis=0) for view in views[2:]
    ]

    tokens_grad = call(
        first_back_body, images,
        [
            (mixed_one_grad, True), (routed, True), (own_mod, True), (grad_one, True),
            (after(picks_row, ada_weight_grad), True), (image_cot, True),
        ],
        [((images, patches, width), BF16)],
    )[0]
    return (
        layer_out.reshape(images * patches, width),
        tokens_grad.reshape(images * patches, width),
        ada_weight_grad,
        ada_bias_grad,
        qkv_weight_grad,
        qv_sum.reshape(2, cols),
        out_weight_grad,
        out_sum,
        up_weight_grad,
        up_bias_grad,
        down_weight_grad,
        down_bias_grad,
    )


def solution(mesh):
    both = ("dp", "mp")
    in_specs = (
        P(both, None), P(both, None), P(both, None), P(both), P(both, None), P(), P(),
        P(None, "mp", None), P(None, "mp"), P("mp", None), P(), P("mp", None), P("mp"),
        P("mp", None), P(),
    )
    out_specs = (
        P(both, None), P(both, None), P(both, None), P(both), P(None, "mp", None), P(None, "mp"),
        P("mp", None), P(), P("mp", None), P("mp"), P("mp", None), P(),
    )

    return jax.shard_map(
        per_device, mesh=mesh, in_specs=in_specs, out_specs=out_specs, check_vma=False
    )
```

```python
import functools
import math

import jax
import jax.numpy as jnp
from jax import lax
from jax.experimental import pallas as pl
from jax.experimental.pallas import tpu as pltpu
from jax.sharding import PartitionSpec as P


HEADS = 16
EPS = 1e-06
F32 = jnp.float32
BF16 = jnp.bfloat16
GELU_A = math.sqrt(2.0 / math.pi)
GELU_B = 0.044715


def norm_rows(rows):
    mean = jnp.mean(rows, axis=-1, keepdims=True)
    centred = rows - mean
    rstd = lax.rsqrt(jnp.mean(centred * centred, axis=-1, keepdims=True) + EPS)
    return centred * rstd, rstd


def norm_back(normed, rstd, grad):
    return rstd * (
        grad
        - jnp.mean(grad, axis=-1, keepdims=True)
        - normed * jnp.mean(grad * normed, axis=-1, keepdims=True)
    )


def mm(left, right, dims=((1,), (0,))):
    return lax.dot_general(left, right, (dims, ((), ())), preferred_element_type=F32)


NT = ((1,), (1,))
TN = ((0,), (0,))


def block(shape):
    rank = len(shape)
    return pl.BlockSpec((1,) + tuple(shape[1:]), lambda i: (i,) + (0,) * (rank - 1))


def whole(shape):
    rank = len(shape)
    return pl.BlockSpec(tuple(shape), lambda i: (0,) * rank)


def call(body, grid, ins, outs, fixed=0, scratch=()):
    moving = len(outs) - fixed
    return pl.pallas_call(
        body,
        grid=(grid,),
        in_specs=[
            pl.BlockSpec(memory_space=pltpu.SMEM)
            if step is None
            else block(a.shape) if step else whole(a.shape)
            for a, step in ins
        ],
        out_specs=[block(shape) for shape, _ in outs[:moving]]
        + [whole(shape) for shape, _ in outs[moving:]],
        scratch_shapes=list(scratch),
        out_shape=[jax.ShapeDtypeStruct(shape, dtype) for shape, dtype in outs],
    )(*[a for a, _ in ins])


def halves_body(side, left, right, own, other, total):
    step, half = left.shape[1], own.shape[0]
    at = pl.multiple_of(pl.program_id(0) * step, step)
    total[pl.ds(at, step), :] = mm(left[...], right[...], TN).astype(BF16)

    @pl.when(pl.program_id(0) == pl.num_programs(0) - 1)
    def _():
        own[...] = total[pl.ds(pl.multiple_of(side[0] * half, half), half), :]
        other[...] = total[pl.ds(pl.multiple_of((1 - side[0]) * half, half), half), :]


def weight_halves(left, right):
    rows, cols = left.shape
    width = right.shape[1]
    step = 384 if cols % 384 == 0 else cols
    half = jax.ShapeDtypeStruct((cols // 2, width), BF16)
    return pl.pallas_call(
        halves_body,
        grid_spec=pltpu.PrefetchScalarGridSpec(
            num_scalar_prefetch=1,
            grid=(cols // step,),
            in_specs=[
                pl.BlockSpec((rows, step), lambda i, p: (0, i)),
                pl.BlockSpec((rows, width), lambda i, p: (0, 0)),
            ],
            out_specs=[pl.BlockSpec((cols // 2, width), lambda i, p: (0, 0))] * 2,
            scratch_shapes=[pltpu.VMEM((cols, width), BF16)],
        ),
        out_shape=[half, half],
    )(jnp.full((1,), lax.axis_index("dp") & 1, jnp.int32), left, right)


def modulate_body(cond, weight, bias, out):
    out[0] = mm(cond[...], weight[0], NT) + bias[0]


def split_call(body, start, images, group, own_ins, group_ins, outs, fixed=(), scratch=()):
    start = jnp.full((1,), start, jnp.int32)
    shapes = [jax.ShapeDtypeStruct(shape, dtype) for shape, dtype in outs]
    apart = [jax.ShapeDtypeStruct(shape, dtype) for shape, dtype in fixed]

    def at(shape, first, moving):
        rest = (0,) * (len(shape) - 1)

        def place(i, p):
            return ((p[0] + first + i) % group if moving else i,) + rest

        return pl.BlockSpec((1,) + tuple(shape[1:]), place)

    def full(shape):
        return pl.BlockSpec(tuple(shape), lambda i, p: (0,) * len(shape))

    def run(ins, first, count, filled, moving):
        def step(index, *refs):
            body(*refs[: len(ins)], *refs[len(ins) + len(filled) :])

        return pl.pallas_call(
            step,
            grid_spec=pltpu.PrefetchScalarGridSpec(
                num_scalar_prefetch=1,
                grid=(count,),
                in_specs=[at(a.shape, first, moving) if by else full(a.shape) for a, by in ins]
                + [pl.BlockSpec(memory_space=pl.ANY)] * len(filled),
                out_specs=[at(one.shape, first, True) for one in shapes]
                + [full(one.shape) for one in apart],
                scratch_shapes=list(scratch),
            ),
            out_shape=shapes + apart,
            input_output_aliases={1 + len(ins) + i: i for i in range(len(filled))},
        )(start, *[a for a, _ in ins], *filled)

    own = run(own_ins, 0, images, [], False)
    rest = run(group_ins, images, group - images, own[: len(shapes)], True)
    return list(rest[: len(shapes)]) + [(a, b) for a, b in zip(own[len(shapes) :], rest[len(shapes) :])]


def gather_body(picks, tokens, cotangent, routed, grad_two):
    slots, patches = routed.shape[1], tokens.shape[1]
    hot = (lax.broadcasted_iota(jnp.int32, (slots, patches), 1) == picks[0]).astype(F32)
    hot = hot.astype(BF16)
    routed[0] = mm(hot, tokens[0]).astype(BF16)
    grad_two[0] = mm(hot, cotangent[0]).astype(BF16)


def mod_row(mod, index):
    return mod[0][index : index + 1, :]


def live_rows(keep, slots):
    return (lax.broadcasted_iota(jnp.int32, (slots, 1), 0).astype(F32) < keep[0][:, :1]).astype(F32)


def live_keys(keep, slots):
    return lax.broadcasted_iota(jnp.int32, (1, slots), 1).astype(F32) < keep[0][:, :1]


def head_mask(head, head_dim, cols):
    lane = lax.broadcasted_iota(jnp.int32, (1, cols), 1)
    inside = jnp.logical_and(lane >= head * head_dim, lane < (head + 1) * head_dim)
    return inside.astype(F32).astype(BF16)


def softmax_of(query, key, alive, scale):
    scores = mm(query, key, NT) * scale
    scores = jnp.where(alive, scores, -1e30)
    raised = jnp.exp(scores - jnp.max(scores, axis=-1, keepdims=True))
    return raised / jnp.sum(raised, axis=-1, keepdims=True)


def attend_body(head_dim, routed, mod, keep, weight, bias, out_weight, mixed, qkv, attended, branch):
    slots, cols = routed.shape[1], weight.shape[1]
    scale = 1.0 / math.sqrt(head_dim)
    normed, _ = norm_rows(routed[0].astype(F32))
    rows = (normed * (1.0 + mod_row(mod, 1)) + mod_row(mod, 0)).astype(BF16)
    mixed[0] = rows
    query = (mm(rows, weight[0], NT) + bias[0:1, :]).astype(BF16)
    key = mm(rows, weight[1], NT).astype(BF16)
    value = (mm(rows, weight[2], NT) + bias[1:2, :]).astype(BF16)
    qkv[0, 0] = query
    qkv[0, 1] = key
    qkv[0, 2] = value
    alive = live_keys(keep, slots)
    total = jnp.zeros((slots, cols), F32)
    for head in range(cols // head_dim):
        mask = head_mask(head, head_dim, cols)
        low = softmax_of(query * mask, key, alive, scale).astype(BF16)
        total = total + mm(low, value * mask)
    total = total.astype(BF16)
    attended[0] = total
    branch[0] = mm(total, out_weight[...]).astype(BF16)


def attend_back_body(
    head_dim, side, grad, qkv, routed, mixed, attended, keep, weight, out_weight,
    mixed_grad, stats, bias_sums, own_part, other_part, kept,
):
    slots, cols = routed.shape[1], weight.shape[1]
    scale = 1.0 / math.sqrt(head_dim)
    here = pl.ds(pl.multiple_of(pl.program_id(0) * slots, slots), slots)
    rows_grad = grad[here, :]
    attended_grad = mm(rows_grad, out_weight[...], NT).astype(BF16)
    query, key, value = qkv[0, 0], qkv[0, 1], qkv[0, 2]
    alive = live_keys(keep, slots)
    query_grad = jnp.zeros((slots, cols), F32)
    key_grad = jnp.zeros((slots, cols), F32)
    value_grad = jnp.zeros((slots, cols), F32)
    for head in range(cols // head_dim):
        mask = head_mask(head, head_dim, cols)
        own_query = query * mask
        weights = softmax_of(own_query, key, alive, scale)
        own_grad = attended_grad * mask
        weight_grad = mm(own_grad, value, NT)
        value_grad = value_grad + mm(weights.astype(BF16), own_grad, TN)
        row_total = jnp.sum(weights * weight_grad, axis=-1, keepdims=True)
        score_grad = (weights * (weight_grad - row_total)).astype(BF16)
        query_grad = query_grad + mm(score_grad, key * mask)
        key_grad = key_grad + mm(score_grad, own_query, TN)
    query_grad = (query_grad * scale).astype(BF16)
    key_grad = (key_grad * scale).astype(BF16)
    value_grad = value_grad.astype(BF16)
    for index, one in enumerate((query_grad, key_grad, value_grad)):
        kept[index, here, :] = one
    rows = mm(query_grad, weight[0]) + mm(key_grad, weight[1]) + mm(value_grad, weight[2])
    mixed_grad[0] = rows.astype(BF16)
    normed, _ = norm_rows(routed[0].astype(F32))
    stats[0, 0:1, :] = jnp.sum(rows, axis=0, keepdims=True)
    stats[0, 1:2, :] = jnp.sum(rows * normed, axis=0, keepdims=True)
    stats[0, 2:3, :] = jnp.sum(rows_grad.astype(F32), axis=0, keepdims=True)
    bias_sums[0, 0:1, :] = jnp.sum(query_grad.astype(F32), axis=0, keepdims=True)
    bias_sums[0, 1:2, :] = jnp.sum(value_grad.astype(F32), axis=0, keepdims=True)

    @pl.when(pl.program_id(0) == pl.num_programs(0) - 1)
    def _():
        def put(index, value):
            @pl.when(side[0] == index // 2)
            def _():
                own_part[index % 2] = value

            @pl.when(side[0] != index // 2)
            def _():
                other_part[index % 2] = value

        def product(index, carry):
            put(index, mm(kept[index], mixed[...], TN).astype(BF16))
            return carry

        lax.fori_loop(0, 3, product, 0)
        put(3, mm(attended[...], grad[...], TN).astype(BF16))


def down_back_body(grad_two, mod, keep, down, down_grad, active_grad, down_sum):
    gate = live_rows(keep, grad_two.shape[1]) * mod_row(mod, 5)
    rows = (gate * grad_two[0].astype(F32)).astype(BF16)
    down_grad[0] = rows
    down_sum[0] = jnp.sum(rows.astype(F32), axis=0, keepdims=True)
    active_grad[0] = mm(rows, down[...], NT)


def forward_body(mixed, active_grad, up, up_bias, active, before_grad, mixed_grad, up_sum):
    units = up.shape[0]
    step = 384 if units % 384 == 0 else units
    rows = mixed[0]
    total = None
    for start in range(0, units, step):
        at = slice(start, start + step)
        before = mm(rows, up[at, :], NT) + up_bias[:, at]
        square = before * before
        tanh = jnp.tanh(GELU_A * (before + GELU_B * (before * square)))
        half = 0.5 * (1.0 + tanh)
        active[0, :, at] = (before * half).astype(BF16)
        slope = half + 0.5 * before * (1.0 - tanh * tanh) * (
            GELU_A * (1.0 + 3.0 * GELU_B * square)
        )
        inner = (active_grad[0, :, at] * slope).astype(BF16)
        before_grad[0, :, at] = inner
        up_sum[0, :, at] = jnp.sum(inner.astype(F32), axis=0, keepdims=True)
        piece = mm(inner, up[at, :])
        total = piece if total is None else total + piece
    mixed_grad[0] = total.astype(BF16)


def branch_body(active, grad_two, keep, down, bias, branch, gate_grad):
    rows = mm(active[0], down[...])
    branch[0] = rows.astype(BF16)
    grad = live_rows(keep, grad_two.shape[1]) * grad_two[0].astype(F32)
    gate_grad[0] = jnp.sum(grad * (rows + bias[...]), axis=0, keepdims=True)


def middle_body(branch, out_bias, routed, mod, keep, hidden, mixed):
    slots = routed.shape[1]
    branch_one = branch[0].astype(F32) + out_bias[...]
    rows = routed[0].astype(F32) + live_rows(keep, slots) * mod_row(mod, 2) * branch_one
    hidden[0] = rows
    normed, _ = norm_rows(rows)
    mixed[0] = (normed * (1.0 + mod_row(mod, 4)) + mod_row(mod, 3)).astype(BF16)


def middle_back_body(
    mixed_grad, hidden, branch, out_bias, grad_two, mod, keep, grad_one, branch_grad, stats
):
    slots = hidden.shape[1]
    rows = mixed_grad[0].astype(F32)
    normed, rstd = norm_rows(hidden[0])
    grad = grad_two[0].astype(F32) + norm_back(normed, rstd, rows * (1.0 + mod_row(mod, 4)))
    grad_one[0] = grad
    live = live_rows(keep, slots)
    branch_one = branch[0].astype(F32) + out_bias[...]
    stats[0, 0:1, :] = jnp.sum(live * grad * branch_one, axis=0, keepdims=True)
    stats[0, 1:2, :] = jnp.sum(rows, axis=0, keepdims=True)
    stats[0, 2:3, :] = jnp.sum(rows * normed, axis=0, keepdims=True)
    branch_grad[0] = (live * mod_row(mod, 2) * grad).astype(BF16)


def place(picks, base, rows):
    patches, slots = base.shape[0], rows.shape[0]
    hot = (lax.broadcasted_iota(jnp.int32, (patches, slots), 0) == picks).astype(F32)
    taken = jnp.max(hot, axis=1, keepdims=True) > 0
    return jnp.where(taken, mm(hot.astype(BF16), rows.astype(BF16)), base.astype(F32)).astype(BF16)


def out_body(branch, hidden, down_bias, mod, keep, picks, tokens, layer_out):
    branch_two = branch[0].astype(F32) + down_bias[...]
    rows = hidden[0] + live_rows(keep, hidden.shape[1]) * mod_row(mod, 5) * branch_two
    layer_out[0] = place(picks[0], tokens[0], rows)


def first_back_body(mixed_grad, routed, mod, grad_one, picks, cotangent, tokens_grad):
    normed, rstd = norm_rows(routed[0].astype(F32))
    rows = mixed_grad[0].astype(F32) * (1.0 + mod_row(mod, 1))
    tokens_grad[0] = place(picks[0], cotangent[0], grad_one[0] + norm_back(normed, rstd, rows))


def dp_bits():
    count = lax.axis_size("dp").bit_length() - 1
    return list(range(count))


def partner(bit):
    return [(i, i ^ (1 << bit)) for i in range(lax.axis_size("dp"))]


def halve(part, bit):
    side = (lax.axis_index("dp") >> bit) & 1
    halves = part.reshape(2, part.shape[0] // 2, part.shape[1])
    own = lax.dynamic_index_in_dim(halves, side, 0, keepdims=False)
    other = lax.dynamic_index_in_dim(halves, 1 - side, 0, keepdims=False)
    return own, lax.ppermute(other, "dp", partner(bit))


def add_low(own, got):
    return (own.astype(F32) + got.astype(F32)).astype(BF16)


def double(part, bit):
    return part, lax.ppermute(part, "dp", partner(bit))


def join(own, got, bit):
    side = (lax.axis_index("dp") >> bit) & 1
    return jnp.where(side == 0, jnp.concatenate([own, got], 0), jnp.concatenate([got, own], 0))


def after(value, *others):
    return lax.optimization_barrier((value,) + others)[0]


def halve_all(parts, level):
    ways = orders()
    flights = [halve(part, way[level]) for part, way in zip(parts, ways)]
    return [add_low(own, got) for own, got in lax.optimization_barrier(flights)]


def double_all(parts, level):
    flights = [double(part, way[level]) for part, way in zip(parts, orders())]
    return lax.optimization_barrier(flights)


def join_all(flights, level):
    return [join(own, got, way[level]) for (own, got), way in zip(flights, orders())]


def trade(part):
    count, mine = lax.axis_size("dp") // 2, lax.axis_index("dp") >> 1
    blocks = part.reshape(count, part.shape[0] // count, part.shape[1])
    own = lax.dynamic_index_in_dim(blocks, mine, 0, keepdims=False)
    sends = [
        lax.dynamic_index_in_dim(blocks, mine ^ step, 0, keepdims=False) for step in range(1, count)
    ]
    return [own] + far(sends)


def far(sends):
    every = range(lax.axis_size("dp"))
    return [
        lax.ppermute(send, "dp", [(i, i ^ (2 * step)) for i in every])
        for step, send in enumerate(sends, 1)
    ]


def spread(block):
    return [block] + far([block] * (lax.axis_size("dp") // 2 - 1))


def finish_body(places, own, got, first, second):
    count, rows = own.shape[0], first.shape[1]
    cut = first.shape[0]
    side, mine = places[0], places[1]

    def block(step):
        place = (step % count) ^ mine
        left, right = own[place, :rows, :], got[place, :rows, :]
        return jnp.where(step // count == side, left, right).astype(F32)

    def fill_first(step, carry):
        first[step] = block(step)
        return carry

    def fill_second(step, carry):
        second[step] = block(step + cut)
        return carry

    lax.fori_loop(0, cut, fill_first, 0)
    lax.fori_loop(0, 2 * count - cut, fill_second, 0)


def finish(own, got, rows):
    count, _, width = own.shape
    index = lax.axis_index("dp")
    places = jnp.stack([index & 1, index >> 1]).astype(jnp.int32)
    cut = 3 * count // 2
    vmem = pl.BlockSpec(memory_space=pltpu.VMEM)
    return pl.pallas_call(
        finish_body,
        in_specs=[pl.BlockSpec(memory_space=pltpu.SMEM), vmem, vmem],
        out_specs=[vmem, vmem],
        out_shape=[
            jax.ShapeDtypeStruct((cut, rows, width), F32),
            jax.ShapeDtypeStruct((2 * count - cut, rows, width), F32),
        ],
        name="finish",
    )(places, own, got)


def orders():
    bits = dp_bits()
    return bits, bits[:1] + bits[2:] + bits[1:2]


def shift(value, step):
    count = lax.axis_size("mp")
    return lax.ppermute(value, "mp", [(i, (i + step) % count) for i in range(count)])


def small_gather(value):
    count, here = lax.axis_size("mp"), lax.axis_index("mp")
    rows = jnp.stack([value] + [shift(value, step) for step in range(1, count)])
    return jnp.take(rows, (here - jnp.arange(count)) % count, axis=0)


def small_scatter_sum(parts):
    count, here = lax.axis_size("mp"), lax.axis_index("mp")
    total = lax.dynamic_index_in_dim(parts, here, 0, keepdims=False)
    for step in range(1, count):
        to = (here + step) % count
        total = total + shift(lax.dynamic_index_in_dim(parts, to, 0, keepdims=False), step)
    return total


def all_rows(rows):
    return lax.all_gather(rows, "mp", axis=0, tiled=True)


def chain_rows(rows):
    count = lax.axis_size("mp")
    up = down = rows
    ups, downs = [], []
    for hop in range(1, count):
        up = lax.ppermute(up, "mp", [(i, i + 1) for i in range(hop - 1, count - 1)])
        down = lax.ppermute(down, "mp", [(i, i - 1) for i in range(count - hop, 0, -1)])
        ups.append(up)
        downs.append(down)
    return ups, downs


def in_order(rows, ups, downs):
    count, here = lax.axis_size("mp"), lax.axis_index("mp")
    slots = [rows] + [
        jnp.where(here > hop, up, down) for hop, (up, down) in enumerate(zip(ups, downs[::-1]))
    ]
    order = (here - jnp.arange(count)) % count
    return jnp.concatenate(
        [lax.dynamic_index_in_dim(jnp.stack(slots), order[i], 0, False) for i in range(count)]
    )


def own_sum(rows):
    return lax.psum_scatter(rows, "mp", scatter_dimension=0, tiled=True)


def per_device(
    tokens, conditioning, routes, keep_count, cotangent, ada_weight, ada_bias, qkv_weight,
    qv_bias, out_weight, out_bias, up_weight, up_bias, down_weight, down_bias,
):
    images = conditioning.shape[0]
    width = tokens.shape[1]
    patches = routes.shape[1]
    slots = 3 * patches // 4
    cols = qkv_weight.shape[1]
    head_dim = width // HEADS
    hidden_units = up_weight.shape[0]
    members = lax.axis_size("mp")
    groups = lax.axis_size("dp")
    group = members * images
    here = lax.axis_index("mp")

    image_tokens = tokens.reshape(images, patches, width)
    image_cot = cotangent.reshape(images, patches, width)
    picks = routes[:, :slots]
    picks_col = picks.reshape(images, slots, 1)
    picks_row = picks.reshape(images, 1, slots)
    rows_shape = (images, slots, width)
    group_shape = (group, slots, width)

    routed, grad_two = call(
        gather_body, images,
        [(picks_col, True), (image_tokens, True), (image_cot, True)],
        [(rows_shape, BF16), (rows_shape, BF16)],
    )
    group_routed = all_rows(routed)
    near = members <= 4
    if near:
        hops = chain_rows(after(grad_two, group_routed))
    else:
        group_two = all_rows(grad_two)

    small = jnp.concatenate(
        [conditioning, jnp.broadcast_to(keep_count.astype(BF16)[:, None], (images, 128))], axis=1
    )
    small = small_gather(small).reshape(group, width + 128)
    silu_cond = jax.nn.silu(small[:, :width].astype(F32)).astype(BF16)
    (modulation,) = call(
        modulate_body, 6,
        [
            (silu_cond, False), (ada_weight.reshape(6, width, width), True),
            (ada_bias.astype(F32).reshape(6, 1, width), True),
        ],
        [((6, group, width), F32)],
    )
    modulation = modulation.transpose(1, 0, 2)
    keep = small[:, None, width:].astype(F32)
    own_mod = lax.dynamic_slice_in_dim(modulation, here * images, images, 0)
    own_keep = jnp.broadcast_to(keep_count.astype(F32)[:, None, None], (images, 1, 128))
    out_bias_row = out_bias.astype(F32)[None]
    down_bias_row = down_bias.astype(F32)[None]

    first_image = here * images
    fixed_ins = [(qkv_weight, False), (qv_bias.astype(F32), False), (out_weight, False)]
    mixed_one, qkv, attended, branch = split_call(
        functools.partial(attend_body, head_dim), first_image, images, group,
        [(routed, True), (own_mod, True), (own_keep, True)] + fixed_ins,
        [(group_routed, True), (modulation, True), (keep, True)] + fixed_ins,
        [
            (group_shape, BF16), ((group, 3, slots, cols), BF16), ((group, slots, cols), BF16),
            (group_shape, BF16),
        ],
    )
    branch_one = own_sum(branch)
    hidden_one, mixed_two = call(
        middle_body, images,
        [
            (branch_one, True), (out_bias_row, False), (routed, True), (own_mod, True),
            (own_keep, True),
        ],
        [(rows_shape, F32), (rows_shape, BF16)],
    )
    group_mixed = all_rows(mixed_two)
    if near:
        group_two = in_order(grad_two, *after(hops, mixed_two))
    unit_shape = (group, slots, hidden_units)
    down_grad, active_grad, down_sum = call(
        down_back_body, group,
        [(group_two, True), (modulation, True), (keep, True), (down_weight, False)],
        [(group_shape, BF16), (unit_shape, F32), ((group, 1, width), F32)],
    )
    own_active_grad = lax.dynamic_slice_in_dim(active_grad, first_image, images, 0)
    fixed_ins = [(up_weight, False), (up_bias.astype(F32)[None], False)]
    active, before_grad, mixed_grad, up_sum = split_call(
        forward_body, first_image, images, group,
        [(mixed_two, True), (own_active_grad, True)] + fixed_ins,
        [(group_mixed, True), (active_grad, True)] + fixed_ins,
        [
            (unit_shape, BF16), (unit_shape, BF16), (group_shape, BF16),
            ((group, 1, hidden_units), F32),
        ],
    )
    mixed_two_grad = own_sum(mixed_grad)
    flat = (group * slots, hidden_units)
    wide = (group * slots, width)
    up_part = weight_halves(before_grad.reshape(flat), group_mixed.reshape(wide))
    down_part = weight_halves(active.reshape(flat), down_grad.reshape(wide))
    levels = len(dp_bits())
    flights = [
        (own, lax.ppermute(other, "dp", partner(0))) for own, other in (up_part, down_part)
    ]
    sums = [add_low(own, got) for own, got in lax.optimization_barrier(flights)]
    branch, gate_grad = call(
        branch_body, group,
        [
            (active, True), (group_two, True), (after(keep, *sums), True), (down_weight, False),
            (jnp.where(here == 0, down_bias_row, 0.0), False),
        ],
        [(group_shape, BF16), ((group, 1, width), F32)],
    )
    sums = halve_all(sums, 1)

    grad_one, branch_grad, middle_stats = call(
        middle_back_body, images,
        [
            (mixed_two_grad, True), (hidden_one, True), (branch_one, True), (out_bias_row, False),
            (grad_two, True), (own_mod, True), (after(own_keep, gate_grad), True),
        ],
        [(rows_shape, F32), (rows_shape, BF16), ((images, 3, width), F32)],
    )
    group_grad = all_rows(branch_grad)
    branch_two = own_sum(branch)
    for level in range(2, levels):
        sums = halve_all(sums, level)
    for level in reversed(range(1, levels)):
        sums = join_all(double_all(sums, level), level)
    last = double_all(sums, 0)
    mixed_grad, attend_stats, bias_sums, own_part, other_part = call(
        functools.partial(attend_back_body, head_dim), group,
        [
            (jnp.full((1,), lax.axis_index("dp") & 1, jnp.int32), None),
            (group_grad.reshape(wide), False), (qkv, True), (group_routed, True),
            (mixed_one.reshape(wide), False), (attended.reshape(-1, cols), False),
            (after(keep, last), True), (qkv_weight, False), (out_weight, False),
        ],
        [
            (group_shape, BF16), ((group, 3, width), F32), ((group, 2, cols), F32),
            ((2, cols, width), BF16), ((2, cols, width), BF16),
        ],
        fixed=2,
        scratch=[pltpu.VMEM((3, group * slots, cols), BF16)],
    )
    (layer_out,) = call(
        out_body, images,
        [
            (branch_two, True), (hidden_one, True), (down_bias_row, False), (own_mod, True),
            (after(own_keep, attend_stats), True), (picks_row, True), (image_tokens, True),
        ],
        [((images, patches, width), BF16)],
    )
    mixed_one_grad = own_sum(mixed_grad)
    other_part = lax.ppermute(other_part.reshape(2 * cols, width), "dp", partner(0))
    half = add_low(own_part.reshape(2 * cols, width), other_part)
    last = after(last, half)
    blocks = trade(half)

    placed = lax.dynamic_update_slice(
        jnp.zeros((group, 3, width), F32), middle_stats, (here * images, 0, 0)
    )
    mod_grad = jnp.concatenate([attend_stats[:, :2], placed, gate_grad], axis=1)
    each = 6 * width // (groups * members)
    mod_grad = mod_grad.reshape(group, groups, members, each)
    mod_grad = small_scatter_sum(mod_grad.transpose(2, 0, 1, 3)).astype(BF16)
    pieces = [
        mod_grad.reshape(-1),
        silu_cond.reshape(-1),
        jnp.sum(bias_sums, axis=0).astype(BF16).reshape(-1),
        jnp.sum(attend_stats[:, 2], axis=0).astype(BF16),
        jnp.sum(up_sum, axis=0).astype(BF16).reshape(-1),
        jnp.sum(down_sum, axis=0).astype(BF16).reshape(-1),
    ]
    sizes = [piece.shape[0] for piece in pieces]
    packed = jnp.concatenate(pieces)
    packed = jnp.pad(packed, (0, -packed.shape[0] % (16 * width))).reshape(-1, width)
    blocks = after(blocks, packed)
    block_sum = sum(one.astype(F32) for one in blocks).astype(BF16)
    rows = block_sum.shape[0]
    last = after(last, block_sum)
    up_weight_grad, down_weight_grad = [one.astype(F32) for one in join_all(last, 0)]
    pieces = spread(jnp.concatenate([block_sum, packed]))
    own = jnp.stack(after(pieces, up_weight_grad, down_weight_grad, layer_out))
    own, got = double(own, 0)
    qkv_weight_grad, out_weight_grad = finish(own, got, rows)
    qkv_weight_grad = qkv_weight_grad.reshape(3, cols, width)
    out_weight_grad = out_weight_grad.reshape(cols, width)

    packed = jnp.stack([own[:, rows:], got[:, rows:]]).reshape(2, groups // 2, -1)
    place = lax.axis_index("dp")
    order = jnp.arange(groups) ^ place
    packed = packed[order & 1, order >> 1]
    starts = [sum(sizes[:i]) for i in range(len(sizes))]
    views = [packed[:, s : s + n] for s, n in zip(starts, sizes)]
    mod_all = views[0].reshape(groups, group, groups, each)
    mod_all = lax.dynamic_index_in_dim(mod_all, lax.axis_index("dp"), 2, keepdims=False)
    mod_all = mod_all.reshape(groups * group, each)
    cond_all = views[1].reshape(groups * group, width)
    ada_weight_grad = mm(mod_all, cond_all, TN)
    ada_bias_grad = jnp.sum(mod_all.astype(F32), axis=0)
    qv_sum, out_sum, up_bias_grad, down_bias_grad = [
        jnp.sum(view.astype(F32), axis=0) for view in views[2:]
    ]

    tokens_grad = call(
        first_back_body, images,
        [
            (mixed_one_grad, True), (routed, True), (own_mod, True), (grad_one, True),
            (after(picks_row, ada_weight_grad), True), (image_cot, True),
        ],
        [((images, patches, width), BF16)],
    )[0]
    return (
        layer_out.reshape(images * patches, width),
        tokens_grad.reshape(images * patches, width),
        ada_weight_grad,
        ada_bias_grad,
        qkv_weight_grad,
        qv_sum.reshape(2, cols),
        out_weight_grad,
        out_sum,
        up_weight_grad,
        up_bias_grad,
        down_weight_grad,
        down_bias_grad,
    )


def solution(mesh):
    both = ("dp", "mp")
    in_specs = (
        P(both, None), P(both, None), P(both, None), P(both), P(both, None), P(), P(),
        P(None, "mp", None), P(None, "mp"), P("mp", None), P(), P("mp", None), P("mp"),
        P("mp", None), P(),
    )
    out_specs = (
        P(both, None), P(both, None), P(both, None), P(both), P(None, "mp", None), P(None, "mp"),
        P("mp", None), P(), P("mp", None), P("mp"), P("mp", None), P(),
    )

    return jax.shard_map(
        per_device, mesh=mesh, in_specs=in_specs, out_specs=out_specs, check_vma=False
    )
```
